256 devices in a mesh: layer: 4 (over y), row: 16 (over z, core), col: 4 (over x).
Axes of the slice: x: 4, y: 4, z: 8, core: 2. Of those that a mesh axis runs over, the one named last changes fastest.
Arguments:
- ancestor: float32 [6144, 6144], P('row', 'col'), may hold values from -6 to 6
- leaf_lower: bfloat16 [4, 8, 6144, 512], P('layer', 'col', 'row'), may hold values from -6 to 6
- leaf_upper: bfloat16 [4, 8, 512, 6144], P('layer', None, 'row', 'col'), may hold values from -6 to 6
- leaf_upper_inv: bfloat16 [4, 8, 512, 512], P('layer', 'col'), may hold values from -1 to 1, as said below
- leaf_lower_inv: bfloat16 [4, 8, 512, 512], P('layer'), may hold values from -1 to 2, as said below
- leaf_pivots: int32 [4, 8, 512], P('layer'), may hold values from 0 to 511, each once within a row
- leaf_tiles: int32 [4, 8, 24, 24], P('layer'), may hold values 0 or 1
- anc_upper_inv: bfloat16 [512, 512], replicated, may hold values from -1 to 1, as said below
- anc_lower_inv: bfloat16 [512, 512], replicated, may hold values from -1 to 2, as said below
- anc_pivots: int32 [512], replicated, may hold values from 0 to 511, each once
- anc_tiles: int32 [24, 24], replicated, may hold values 0 or 1
Outputs:
- anc_lower: bfloat16 [6144, 512], P('row')
- anc_upper: bfloat16 [512, 6144], P(None, 'col')
- schur: float32 [6144, 6144], P('row', 'col')
The draws below stay inside these ranges and needn't reach their ends.
Inputs may be any that keep to these rules, and one draw needn't show every extreme that they name: leaf_upper_inv[l,k] is upper triangular with positive diagonal. leaf_lower_inv[l,k] is lower triangular with positive diagonal. `anc_upper_inv`: upper triangular with positive diagonal. `anc_lower_inv`: lower triangular with positive diagonal.
All inputs are finite; a program needn't handle non-finite values. No bound on the sum of `leaf_tiles` on one device may be relied on, other than what follows from the above.
Results may differ from the reference program's by a relative error of at most 0.0085.
Values may be sent and summed in bfloat16 or wider, within the bound.
A program may use at most 128 MiB of HBM per device.

```python
import jax
import jax.numpy as jnp

NA = 6144
W = 512
TB = 256
LAYERS = 4
LEAVES = 8
RB = 384
PB = 32
NT = 24


def triangle(key, lead, lower_side):
    first, second = jax.random.split(key)
    shape = lead + (W, W)
    offdiag = jnp.clip(jax.random.normal(first, shape, jnp.float32), -6.0, 6.0)
    diagonal = jnp.exp(jax.random.uniform(second, lead + (W,), jnp.float32, jnp.log(0.5), jnp.log(2.0)))
    identity = jnp.eye(W, dtype=jnp.float32)
    if lower_side:
        matrix = jnp.tril(offdiag, -1) / jnp.sqrt(W * 1.0) + diagonal[..., None] * identity
    else:
        matrix = jnp.triu(offdiag, 1) / (W * 1.0) + diagonal[..., None] * identity / jnp.sqrt(W * 1.0)
    return matrix.astype(jnp.bfloat16)


def draw_leaf_upper_inv(key, part):
    return triangle(jax.random.fold_in(key, 11), (LAYERS, LEAVES), False)


def draw_leaf_lower_inv(key, part):
    return triangle(jax.random.fold_in(key, 12), (LAYERS, LEAVES), True)


def draw_anc_upper_inv(key, part):
    return triangle(jax.random.fold_in(key, 13), (), False)


def draw_anc_lower_inv(key, part):
    return triangle(jax.random.fold_in(key, 14), (), True)


def set_ends(values, own_key, least, largest):
    spot = [jax.random.randint(jax.random.fold_in(own_key, axis), (), 0, length) for axis, length in enumerate(values.shape)]
    main_axis = values.shape.index(max(values.shape))
    next_to = spot[:main_axis] + [(spot[main_axis] + 1) % values.shape[main_axis]] + spot[main_axis + 1:]
    return values.at[tuple(spot)].set(least).at[tuple(next_to)].set(largest)


def levels(rng, shape, pieces, smallest, top_value):
    def one(axis_at, shards_of):
        heights = jax.random.uniform(jax.random.fold_in(jax.random.fold_in(rng, 6), axis_at), (shards_of,), jnp.float32, smallest / len(pieces), top_value / len(pieces))
        return jnp.repeat(jnp.exp(heights), shape[axis_at] // shards_of).reshape((-1,) + (1,) * (len(shape) - axis_at - 1))

    factor_of = one(*pieces[0])
    for cut in pieces[1:]:
        factor_of = factor_of * one(*cut)
    return factor_of


def normal_values(stream_key, extent, scale, limit, pieces=(), kind=jnp.bfloat16):
    entries = scale * jax.random.normal(stream_key, extent, jnp.float32)
    if pieces:
        entries = entries * levels(stream_key, extent, pieces, -0.22, 0.18)
    return jnp.clip(entries, -limit, limit).astype(kind)


def setup_inputs(seed: int = 0) -> dict:
    arg_keys = jax.random.split(jax.random.key(seed), 12)
    ancestor = normal_values(arg_keys[0], (NA, NA), 1.0, 6.0, ((0, 16), (1, 4)), jnp.float32)
    leaf_lower = normal_values(arg_keys[1], (LAYERS, LEAVES, NA, W), 1.0, 6.0, ((0, 4), (1, 4), (2, 16)))
    leaf_upper = normal_values(arg_keys[2], (LAYERS, LEAVES, W, NA), 1.0, 6.0, ((0, 4), (2, 16), (3, 4)))
    leaf_upper_inv = draw_leaf_upper_inv(jax.random.fold_in(arg_keys[11], 71), 0)
    leaf_lower_inv = draw_leaf_lower_inv(jax.random.fold_in(arg_keys[11], 71), 0)
    leaf_pivots = jax.vmap(lambda own: jax.random.permutation(own, W))(jax.random.split(arg_keys[5], LAYERS * LEAVES)).reshape((LAYERS, LEAVES, W)).astype(jnp.int32)
    leaf_tiles = set_ends((jax.random.randint(arg_keys[6], (LAYERS, LEAVES, NT, NT), 0, 2) < 1).astype(jnp.int32), jax.random.fold_in(arg_keys[6], 1), 0, 1)
    anc_upper_inv = draw_anc_upper_inv(jax.random.fold_in(arg_keys[11], 71), 0)
    anc_lower_inv = draw_anc_lower_inv(jax.random.fold_in(arg_keys[11], 71), 0)
    anc_pivots = jax.random.permutation(arg_keys[9], W).astype(jnp.int32)
    anc_tiles = set_ends((jax.random.randint(arg_keys[10], (NT, NT), 0, 2) < 1).astype(jnp.int32), jax.random.fold_in(arg_keys[10], 1), 0, 1)
    return {"ancestor": ancestor, "leaf_lower": leaf_lower, "leaf_upper": leaf_upper, "leaf_upper_inv": leaf_upper_inv, "leaf_lower_inv": leaf_lower_inv, "leaf_pivots": leaf_pivots, "leaf_tiles": leaf_tiles, "anc_upper_inv": anc_upper_inv, "anc_lower_inv": anc_lower_inv, "anc_pivots": anc_pivots, "anc_tiles": anc_tiles}


def tile_mask(tiles):
    expanded = jnp.repeat(jnp.repeat(tiles, TB, axis=0), TB, axis=1)
    return expanded.astype(jnp.float32)


def reference(ancestor, leaf_lower, leaf_upper, leaf_upper_inv, leaf_lower_inv, leaf_pivots, leaf_tiles, anc_upper_inv, anc_lower_inv, anc_pivots, anc_tiles):
    total = jnp.zeros((NA, NA), jnp.float32)
    for layer_index in range(LAYERS):
        for leaf_index in range(LEAVES):
            lower = jnp.dot(leaf_lower[layer_index, leaf_index], leaf_upper_inv[layer_index, leaf_index], preferred_element_type=jnp.float32).astype(jnp.bfloat16)
            permuted = jnp.take(leaf_upper[layer_index, leaf_index], leaf_pivots[layer_index, leaf_index], axis=0)
            upper = jnp.dot(leaf_lower_inv[layer_index, leaf_index], permuted, preferred_element_type=jnp.float32).astype(jnp.bfloat16)
            update = jnp.dot(lower, upper, preferred_element_type=jnp.float32)
            total = total + tile_mask(leaf_tiles[layer_index, leaf_index]) * update
    a_sum = ancestor + total
    blocks = NA // RB
    row_index = (jnp.arange(blocks, dtype=jnp.int32)[:, None] * RB + jnp.arange(PB, dtype=jnp.int32)[None, :]).reshape(-1)
    pivot_rows = jnp.take(a_sum, row_index, axis=0).astype(jnp.bfloat16)
    permuted = jnp.take(pivot_rows, anc_pivots, axis=0)
    anc_upper = jnp.dot(anc_lower_inv, permuted, preferred_element_type=jnp.float32).astype(jnp.bfloat16)
    columns = a_sum[:, :W].astype(jnp.bfloat16)
    anc_lower = jnp.dot(columns, anc_upper_inv, preferred_element_type=jnp.float32).astype(jnp.bfloat16)
    schur = a_sum - tile_mask(anc_tiles) * jnp.dot(anc_lower, anc_upper, preferred_element_type=jnp.float32)
    return anc_lower, anc_upper, schur
```

```python
import jax
import jax.numpy as jnp
from jax import lax
from jax.experimental import pallas as pl
from jax.experimental.pallas import tpu as pltpu
from jax.sharding import PartitionSpec as P

MESH = pl.DeviceIdType.MESH
F32 = jnp.float32
BF = jnp.bfloat16
W = 512
TB = 256
LEAVES = 8
NL = 4
NR = 16
NX = 4
RB = 384
PB = 32
CB = 1536
CW = 256
NC = CB // CW
OWN = RB // NL
ZS = 7


def kernel(
    anc,
    ll,
    lu,
    lui,
    lli,
    piv,
    tiles,
    aui,
    ali,
    apiv,
    atiles,
    o_low,
    o_up,
    o_sch,
    ubuf,
    mbuf,
    v_ll,
    v_lui,
    v_lli,
    v_aui,
    v_ali,
    v_alip,
    v_piv,
    v_apiv,
    v_anc,
    part,
    pst,
    rrecv,
    asum,
    pvt,
    v_low,
    v_up,
    v_sch,
    s_tiles,
    s_atiles,
    in_sem,
    own_sem,
    z_ss,
    z_rs,
    d_ss,
    d_rs,
    x_ss,
    x_rs,
    r_ss,
    r_rs,
    a_ss,
    a_rs,
    p_ss,
    p_rs,
    q_ss,
    q_rs,
    l_ss,
    l_rs,
    out_sem,
):
    l = lax.axis_index("layer")
    r = lax.axis_index("row")
    x = lax.axis_index("col")

    def row_of(step):
        return lax.rem(r + (2 * step + 2 * NR), NR)

    z_dev = {1: (l, row_of(1), x), -1: (l, row_of(-1), x)}
    partner = (l, r + 1 - 2 * lax.rem(r, 2), x)

    def layer_of(d):
        return lax.rem(l + d, NL)

    def col_of(d):
        return lax.rem(x + d + NX, NX)

    loads = {}

    def load(name, src, dst, index):
        loads[name] = pltpu.make_async_copy(src, dst, in_sem.at[index])
        loads[name].start()

    for c in range(NC):
        cp = pltpu.make_async_copy(
            lu.at[0, :, :, pl.ds(c * CW, CW)],
            ubuf.at[c, :, pl.ds(pl.multiple_of(r * PB, PB), PB), :],
            own_sem.at[c],
        )
        cp.start()
        loads[("own", c)] = cp
    load("ll", ll.at[0], v_ll, 0)
    load("lui", lui.at[0], v_lui, 1)
    load("lli", lli.at[0, pl.ds(2 * x, 2)], v_lli, 2)
    load("piv", piv.at[0], v_piv, 3)
    load("tiles", tiles.at[0], s_tiles, 4)
    load("aui", aui, v_aui, 5)
    load("ali", ali, v_ali, 6)
    load("apiv", apiv, v_apiv, 7)
    load("atiles", atiles, s_atiles, 8)
    load("anc", anc.at[pl.ds(pl.multiple_of(l * OWN, OWN), OWN), :], v_anc, 9)

    barrier = pltpu.get_barrier_semaphore()
    others = [z_dev[1], z_dev[-1], partner]
    others += [(layer_of(d), r, x) for d in (1, 2, 3)]
    others += [(l, r, col_of(d)) for d in (1, 2, 3)]
    for dev in others:
        pl.semaphore_signal(barrier, inc=1, device_id=dev, device_id_type=MESH)
    pl.semaphore_wait(barrier, len(others))

    sent = []

    def send(src, dst, ss, rs, dev):
        cp = pltpu.make_async_remote_copy(
            src_ref=src, dst_ref=dst, send_sem=ss, recv_sem=rs, device_id=dev, device_id_type=MESH
        )
        cp.start()
        sent.append(cp)
        return cp

    zc = {}
    dc = {}

    def block(b):
        return pl.ds(pl.multiple_of(b * PB, PB), PB)

    def z_half(s, dr):
        return s % 2 if dr > 0 else 1 - s % 2

    def z_send(c, s):
        for dr in (1, -1):
            i = 0 if dr > 0 else 1
            if s >= 2:
                zc[c, dr, s - 2].wait_recv()
            h = z_half(s, dr)
            b = row_of(-dr * (s // 2))
            dst = ubuf.at[c, pl.ds(4 * h, 4), block(b), :]
            src = lu.at[0, pl.ds(4 * h, 4), :, pl.ds(c * CW, CW)] if s < 2 else dst
            zc[c, dr, s] = send(src, dst, z_ss.at[c, i, s], z_rs.at[c, i, s], z_dev[dr])
        if s == 0:
            d_send(c, 0, 0)
        if s in (3, 5):
            d_send(c, s // 2, 1)
            d_send(c, s // 2, -1)

    def d_send(c, hop, dr):
        i = 0 if hop == 0 else (7 if hop == 4 else 2 * hop - 1 + (dr < 0))
        b = row_of(-dr * hop)
        dst = ubuf.at[c, :, block(b), :]
        src = lu.at[0, :, :, pl.ds(c * CW, CW)] if hop == 0 else dst
        dc[c, i] = send(src, dst, d_ss.at[c, i], d_rs.at[c, i], partner)

    def z_last(c, s):
        for dr in (1, -1):
            zc[c, dr, s].wait_recv()
        if s == 5:
            d_send(c, 3, 1)
            d_send(c, 3, -1)
        else:
            d_send(c, 4, 1)

    xc = {}

    def onehot_rows(row_vector):
        rows = lax.broadcasted_iota(jnp.int32, (W, W), 0)
        return jnp.where(rows == row_vector, 1.0, 0.0).astype(BF)

    def times_t(a, b):
        return lax.dot_general(a, b, (((1,), (1,)), ((), ())), preferred_element_type=F32)

    def left_factor(j):
        if j == 0:
            for name in ("ll", "lui", "lli", "piv"):
                loads[name].wait()
        k = 2 * x + j
        lower = jnp.dot(v_ll[j], v_lui[j], preferred_element_type=F32).astype(BF)
        both = jnp.dot(lower, v_lli[j], preferred_element_type=F32).astype(BF)
        mbuf[k] = times_t(both, onehot_rows(v_piv[pl.ds(k, 1), :])).astype(BF)
        if j == 1:
            x_send(-1, 0, k)
            x_send(-1, 1, k - 1)
        x_send(1, j, k)

    def x_send(dr, slot, k):
        i = 0 if dr > 0 else 1
        ref = mbuf.at[k]
        xc[dr, slot] = send(ref, ref, x_ss.at[i, slot], x_rs.at[i, slot], (l, r, col_of(dr)))

    def x_relay():
        xc[1, 0].wait_recv()
        x_send(1, 2, 2 * col_of(-1))
        xc[-1, 0].wait_recv()
        x_send(-1, 2, 2 * col_of(1) + 1)

    def x_done():
        for dr in (1, -1):
            for slot in (1, 2):
                xc[dr, slot].wait_recv()

    def anc_left():
        loads["ali"].wait()
        loads["apiv"].wait()
        v_alip[...] = times_t(v_ali[...], onehot_rows(v_apiv[...])).astype(BF)

    def ready(c):
        for i in range(8):
            dc[c, i].wait_recv()
        loads["own", c].wait()

    def products(c, first, count):
        def one(k, carry):
            prod = jnp.dot(mbuf[k], ubuf[c, k], preferred_element_type=F32)
            for p in range(3):
                tile = s_tiles[k, (3 * r + p) // 2, NC * x + c].astype(F32)
                rows = slice(128 * p, 128 * p + 128)
                part[c, rows, :] = part[c, rows, :] + tile * prod[rows, :]
            return carry

        if first == 0:
            part[c] = jnp.zeros((RB, CW), F32)
        lax.fori_loop(first, first + count, one, 0)

    rc = {}
    ac = {}

    def own_rows(layer):
        return pl.ds(pl.multiple_of(layer * OWN, OWN), OWN)

    def scatter(c):
        pst[c] = part[c].astype(BF)
        for d in (2, 1, 3):
            to = layer_of(d)
            rc[c, d] = send(
                pst.at[c, own_rows(to), :], rrecv.at[c, d - 1], r_ss.at[c, d - 1], r_rs.at[c, d - 1], (to, r, x)
            )

    def add_up(c):
        if c == 0:
            loads["anc"].wait()
        for d in (1, 2, 3):
            rc[c, d].wait_recv()
        total = part[c, own_rows(l), :] + v_anc[:, c * CW : c * CW + CW]
        for d in range(3):
            total = total + rrecv[c, d].astype(F32)
        asum[c, own_rows(l), :] = total.astype(BF)
        ref = asum.at[c, own_rows(l), :]
        for d in (2, 1, 3):
            ac[c, d] = send(ref, ref, a_ss.at[c, d - 1], a_rs.at[c, d - 1], (layer_of(d), r, x))

    pc = {}
    qc = {}

    def p_send(c, hop, dr):
        i = 0 if dr > 0 else 1
        b = row_of(-dr * hop)
        dst = pvt.at[c, block(b), :]
        src = asum.at[c, pl.ds(0, PB), :] if hop == 0 else dst
        pc[c, dr, hop] = send(src, dst, p_ss.at[c, i, hop], p_rs.at[c, i, hop], z_dev[dr])

    def q_send(c, hop, dr):
        i = 0 if hop == 0 else 2 * hop - 1 + (dr < 0)
        b = row_of(-dr * hop)
        dst = pvt.at[c, block(b), :]
        src = asum.at[c, pl.ds(0, PB), :] if hop == 0 else dst
        qc[c, i] = send(src, dst, q_ss.at[c, i], q_rs.at[c, i], partner)

    def pivots(c, hop):
        if hop == 0:
            for d in (1, 2, 3):
                ac[c, d].wait_recv()
            p_send(c, 0, 1)
            p_send(c, 0, -1)
            q_send(c, 0, 0)
            pvt[c, block(r), :] = asum[c, 0:PB, :]
            return
        for dr in (1, -1):
            if hop == 4 and dr < 0:
                continue
            pc[c, dr, hop - 1].wait_recv()
            if hop < 3 or (hop == 3 and dr > 0):
                p_send(c, hop, dr)
            q_send(c, hop, dr)

    def anc_low():
        loads["aui"].wait()

        @pl.when(x == 0)
        def _():
            low = jnp.dot(asum[0], v_aui[0:CW, :], preferred_element_type=F32)
            low = low + jnp.dot(asum[1], v_aui[CW : 2 * CW, :], preferred_element_type=F32)
            v_low[...] = low.astype(BF)
            for d in (2, 1, 3):
                low_copy(d).start()

    def low_copy(d):
        return pltpu.make_async_remote_copy(
            src_ref=v_low,
            dst_ref=v_low,
            send_sem=l_ss.at[d - 1],
            recv_sem=l_rs,
            device_id=(l, r, col_of(d)),
            device_id_type=MESH,
        )

    def low_done():
        @pl.when(x != 0)
        def _():
            low_copy(1).wait_recv()

        @pl.when(x == 0)
        def _():
            for d in (1, 2, 3):
                low_copy(d).wait_send()

        put(v_low, o_low)

    outs = []

    def put(src, dst):
        cp = pltpu.make_async_copy(src, dst, out_sem.at[len(outs)])
        cp.start()
        outs.append(cp)

    def finish(c):
        for i in range(8):
            qc[c, i].wait_recv()
        v_up[c] = jnp.dot(v_alip[...], pvt[c], preferred_element_type=F32).astype(BF)
        put(v_up.at[c], o_up.at[:, pl.ds(c * CW, CW)])
        prod = jnp.dot(v_low[...], v_up[c], preferred_element_type=F32)
        for p in range(3):
            tile = s_atiles[(3 * r + p) // 2, NC * x + c].astype(F32)
            rows = slice(128 * p, 128 * p + 128)
            v_sch[c, rows, :] = asum[c, rows, :].astype(F32) - tile * prod[rows, :]
        put(v_sch.at[c], o_sch.at[:, pl.ds(c * CW, CW)])

    def comp(c, part_index):
        if part_index == 0:
            ready(c)
            products(c, 0, 4)
        else:
            products(c, 4, 4)
            scatter(c)

    def m_ready():
        x_done()
        loads["tiles"].wait()

    events = {}

    def at(g, fn, *args):
        events.setdefault(g, []).append((fn, args))

    at(1, left_factor, 0)
    at(2, left_factor, 1)
    at(5, anc_left)
    at(10, x_relay)
    at(20, m_ready)
    for c, g in ((0, 20), (1, 22), (2, 24), (3, 30), (4, 37)):
        at(g, comp, c, 0)
        at(g + 1, comp, c, 1)
    for c, g in ((0, 25), (1, 27), (2, 29), (3, 35), (4, 41)):
        at(g, add_up, c)
    for c, g in ((0, 29), (1, 31), (2, 33), (3, 37)):
        for hop in range(5):
            at(g + hop, pivots, c, hop)
    at(31, anc_low)

    for c in range(NC):
        for s in range(ZS):
            z_send(c, s)
            if c > 0 and s < 2:
                z_last(c - 1, 5 + s)
            for fn, args in events.get(ZS * c + s, []):
                fn(*args)
    loads["atiles"].wait()
    c = NC - 1
    z_last(c, 5)
    z_last(c, 6)
    comp(c, 0)
    comp(c, 1)
    pivots(c - 1, 0)
    low_done()
    finish(0)
    pivots(c - 1, 1)
    finish(1)
    pivots(c - 1, 2)
    add_up(c)
    pivots(c - 1, 3)
    finish(2)
    pivots(c - 1, 4)
    pivots(c, 0)
    finish(3)
    for hop in range(1, 5):
        pivots(c, hop)
        if hop == 1:
            finish(4)
    finish(c)
    for cp in sent:
        cp.wait_send()
    for cp in outs:
        cp.wait()


def shards(*args):
    any_space = pl.BlockSpec(memory_space=pl.ANY)
    dma = pltpu.SemaphoreType.DMA
    vmem = pltpu.VMEM
    return pl.pallas_call(
        kernel,
        out_shape=(
            jax.ShapeDtypeStruct((RB, W), BF),
            jax.ShapeDtypeStruct((W, CB), BF),
            jax.ShapeDtypeStruct((RB, CB), F32),
        ),
        in_specs=[any_space] * 11,
        out_specs=(any_space,) * 3,
        scratch_shapes=[
            vmem((NC, LEAVES, W, CW), BF),
            vmem((LEAVES, RB, W), BF),
            vmem((2, RB, W), BF),
            vmem((2, W, W), BF),
            vmem((2, W, W), BF),
            vmem((W, W), BF),
            vmem((W, W), BF),
            vmem((W, W), BF),
            vmem((LEAVES, W), jnp.int32),
            vmem((1, W), jnp.int32),
            vmem((OWN, CB), F32),
            vmem((NC, RB, CW), F32),
            vmem((NC, RB, CW), BF),
            vmem((NC, 3, OWN, CW), BF),
            vmem((NC, RB, CW), BF),
            vmem((NC, W, CW), BF),
            vmem((RB, W), BF),
            vmem((NC, W, CW), BF),
            vmem((NC, RB, CW), F32),
            pltpu.SMEM((LEAVES, 24, 24), jnp.int32),
            pltpu.SMEM((24, 24), jnp.int32),
            dma((10,)),
            dma((NC,)),
            dma((NC, 2, ZS)),
            dma((NC, 2, ZS)),
            dma((NC, 8)),
            dma((NC, 8)),
            dma((2, 3)),
            dma((2, 3)),
            dma((NC, 3)),
            dma((NC, 3)),
            dma((NC, 3)),
            dma((NC, 3)),
            dma((NC, 2, 4)),
            dma((NC, 2, 4)),
            dma((NC, 8)),
            dma((NC, 8)),
            dma((3,)),
            dma(()),
            dma((2 * NC + 1,)),
        ],
        compiler_params=pltpu.CompilerParams(
            collective_id=0, has_side_effects=True, vmem_limit_bytes=56 * 2**20
        ),
    )(*args[:9], args[9].reshape(1, W), args[10])


def solution(mesh):
    return jax.shard_map(
        shards,
        mesh=mesh,
        in_specs=(
            P("row", "col"),
            P("layer", "col", "row", None),
            P("layer", None, "row", "col"),
            P("layer", "col", None, None),
            P("layer", None, None, None),
            P("layer", None, None),
            P("layer", None, None, None),
            P(),
            P(),
            P(),
            P(),
        ),
        out_specs=(P("row", None), P(None, "col"), P("row", "col")),
        check_vma=False,
    )
```

```python
import jax
import jax.numpy as jnp
from jax import lax
from jax.experimental import pallas as pl
from jax.experimental.pallas import tpu as pltpu
from jax.sharding import PartitionSpec as P

MESH = pl.DeviceIdType.MESH
F32 = jnp.float32
BF = jnp.bfloat16
W = 512
TB = 256
LEAVES = 8
NL = 4
NR = 16
NX = 4
RB = 384
PB = 32
CB = 1536
CW = 256
NC = CB // CW
OWN = RB // NL
GAP = 4


def ring_order():
    left = [(c, h, i) for c in range(NC) for h in range(4) for i in range(2) if h < 3 or i == 0]
    order, place = [], {}
    while left:
        g = len(order)
        fit = [m for m in left if m[1] == 0 or place.get((m[0], m[1] - 1, m[2]), g) + GAP <= g]
        order.append(fit[0] if fit else None)
        if fit:
            place[fit[0]] = g
            left.remove(fit[0])
    return order, place


ORDER, PLACE = ring_order()


def kernel(
    anc,
    ll,
    lu,
    lui,
    lli,
    piv,
    tiles,
    aui,
    ali,
    apiv,
    atiles,
    v_low,
    v_up,
    v_sch,
    ubuf,
    mbuf,
    v_ll,
    v_lui,
    v_lli,
    v_aui,
    v_ali,
    v_alip,
    v_piv,
    v_apiv,
    v_anc,
    part,
    pst,
    rrecv,
    asum,
    pvt,
    v_top,
    precv,
    s_tiles,
    s_atiles,
    in_sem,
    own_sem,
    z_ss,
    z_rs,
    d_ss,
    d_rs,
    x_ss,
    x_rs,
    r_ss,
    r_rs,
    a_ss,
    a_rs,
    p_ss,
    p_rs,
    q_ss,
    q_rs,
    l_ss,
    l_rs,
    v_ss,
    v_rs,
):
    l = lax.axis_index("layer")
    r = lax.axis_index("row")
    x = lax.axis_index("col")

    def row_of(step):
        return lax.rem(r + (2 * step + 2 * NR), NR)

    z_dev = {1: (l, row_of(1), x), -1: (l, row_of(-1), x)}
    partner = (l, r + 1 - 2 * lax.rem(r, 2), x)

    def layer_of(d):
        return lax.rem(l + d, NL)

    def col_of(d):
        return lax.rem(x + d + NX, NX)

    loads = {}

    def load(name, src, dst, index):
        loads[name] = pltpu.make_async_copy(src, dst, in_sem.at[index])
        loads[name].start()

    for c in range(NC):
        cp = pltpu.make_async_copy(
            lu.at[0, :, :, pl.ds(c * CW, CW)],
            ubuf.at[c, :, pl.ds(pl.multiple_of(r * PB, PB), PB), :],
            own_sem.at[c],
        )
        cp.start()
        loads[("own", c)] = cp
    load("ll", ll.at[0], v_ll, 0)
    load("lui", lui.at[0], v_lui, 1)
    load("lli", lli.at[0, pl.ds(2 * x, 2)], v_lli, 2)
    load("piv", piv.at[0], v_piv, 3)
    load("tiles", tiles.at[0], s_tiles, 4)
    load("aui", aui, v_aui, 5)
    load("ali", ali, v_ali, 6)
    load("apiv", apiv, v_apiv, 7)
    load("atiles", atiles, s_atiles, 8)
    load("top", anc.at[pl.ds(0, PB), :], v_top, 10)
    load("anc", anc.at[pl.ds(pl.multiple_of(l * OWN, OWN), OWN), :], v_anc, 9)

    barrier = pltpu.get_barrier_semaphore()
    others = [z_dev[1], z_dev[-1], partner]
    others += [(layer_of(d), r, x) for d in (1, 2, 3)]
    others += [(l, r, col_of(d)) for d in (1, 2, 3)]
    for dev in others:
        pl.semaphore_signal(barrier, inc=1, device_id=dev, device_id_type=MESH)
    pl.semaphore_wait(barrier, len(others))

    sent = []

    def send(src, dst, ss, rs, dev):
        cp = pltpu.make_async_remote_copy(
            src_ref=src, dst_ref=dst, send_sem=ss, recv_sem=rs, device_id=dev, device_id_type=MESH
        )
        cp.start()
        sent.append(cp)
        return cp

    zc = {}
    dc = {}

    def block(b):
        return pl.ds(pl.multiple_of(b * PB, PB), PB)

    def z_send(c, hop, i):
        for dr in (1, -1):
            n = 0 if dr > 0 else 1
            if hop:
                zc[c, dr, hop - 1, i].wait_recv()
            h = i if dr > 0 else 1 - i
            dst = ubuf.at[c, pl.ds(4 * h, 4), block(row_of(-dr * hop)), :]
            src = lu.at[0, pl.ds(4 * h, 4), :, pl.ds(c * CW, CW)] if hop == 0 else dst
            slot = 2 * hop + i
            zc[c, dr, hop, i] = send(src, dst, z_ss.at[c, n, slot], z_rs.at[c, n, slot], z_dev[dr])
        if hop == 0 and i == 0:
            d_send(c, 0, 0)
        if hop in (1, 2) and i == 1:
            d_send(c, hop, 1)
            d_send(c, hop, -1)

    def d_send(c, hop, dr):
        i = 0 if hop == 0 else (7 if hop == 4 else 2 * hop - 1 + (dr < 0))
        b = row_of(-dr * hop)
        dst = ubuf.at[c, :, block(b), :]
        src = lu.at[0, :, :, pl.ds(c * CW, CW)] if hop == 0 else dst
        dc[c, i] = send(src, dst, d_ss.at[c, i], d_rs.at[c, i], partner)

    def z_last(c, hop):
        for dr in (1, -1):
            zc[c, dr, hop, 1 if hop == 2 else 0].wait_recv()
        if hop == 2:
            d_send(c, 3, 1)
            d_send(c, 3, -1)
        else:
            d_send(c, 4, 1)

    xc = {}

    def onehot_rows(row_vector):
        rows = lax.broadcasted_iota(jnp.int32, (W, W), 0)
        return jnp.where(rows == row_vector, 1.0, 0.0).astype(BF)

    def times_t(a, b):
        return lax.dot_general(a, b, (((1,), (1,)), ((), ())), preferred_element_type=F32)

    def left_factor(j):
        if j == 0:
            for name in ("ll", "lui", "lli", "piv"):
                loads[name].wait()
        k = 2 * x + j
        lower = jnp.dot(v_ll[j], v_lui[j], preferred_element_type=F32).astype(BF)
        both = jnp.dot(lower, v_lli[j], preferred_element_type=F32).astype(BF)
        mbuf[k] = times_t(both, onehot_rows(v_piv[pl.ds(k, 1), :])).astype(BF)
        if j == 1:
            x_send(-1, 0, k)
            x_send(-1, 1, k - 1)
        x_send(1, j, k)

    def x_send(dr, slot, k):
        i = 0 if dr > 0 else 1
        ref = mbuf.at[k]
        xc[dr, slot] = send(ref, ref, x_ss.at[i, slot], x_rs.at[i, slot], (l, r, col_of(dr)))

    def x_relay():
        xc[1, 0].wait_recv()
        x_send(1, 2, 2 * col_of(-1))
        xc[-1, 0].wait_recv()
        x_send(-1, 2, 2 * col_of(1) + 1)

    def x_done():
        for dr in (1, -1):
            for slot in (1, 2):
                xc[dr, slot].wait_recv()

    def anc_left():
        loads["ali"].wait()
        loads["apiv"].wait()
        v_alip[...] = times_t(v_ali[...], onehot_rows(v_apiv[...])).astype(BF)

    def ready(c):
        for i in range(8):
            dc[c, i].wait_recv()
        loads["own", c].wait()

    def products(c, p):
        rows = slice(128 * p, 128 * p + 128)
        total = None
        for k in range(LEAVES):
            tile = s_tiles[k, (3 * r + p) // 2, NC * x + c].astype(F32)
            prod = tile * jnp.dot(mbuf[k, rows, :], ubuf[c, k], preferred_element_type=F32)
            total = prod if total is None else total + prod
        part[c, rows, :] = total
        pst[c, rows, :] = total.astype(BF)

    rc = {}
    ac = {}

    def own_rows(layer):
        return pl.ds(pl.multiple_of(layer * OWN, OWN), OWN)

    def scatter(c):
        for d in (2, 1, 3):
            to = layer_of(d)
            rc[c, d] = send(
                pst.at[c, own_rows(to), :], rrecv.at[c, d - 1], r_ss.at[c, d - 1], r_rs.at[c, d - 1], (to, r, x)
            )

    def add_up(c):
        if c == 0:
            loads["anc"].wait()
        for d in (1, 2, 3):
            rc[c, d].wait_recv()
        total = part[c, own_rows(l), :] + v_anc[:, c * CW : c * CW + CW]
        for d in range(3):
            total = total + rrecv[c, d].astype(F32)
        asum[c, own_rows(l), :] = total.astype(BF)
        ref = asum.at[c, own_rows(l), :]
        for d in (2, 1, 3):
            ac[c, d] = send(ref, ref, a_ss.at[c, d - 1], a_rs.at[c, d - 1], (layer_of(d), r, x))

    def gathered(c):
        if c not in done:
            done.add(c)
            for d in (1, 2, 3):
                ac[c, d].wait_recv()

    done = set()

    pc = {}
    qc = {}

    def p_send(c, hop, dr):
        i = 0 if dr > 0 else 1
        b = row_of(-dr * hop)
        ref = pvt.at[c, block(b), :]
        pc[c, dr, hop] = send(ref, ref, p_ss.at[c, i, hop], p_rs.at[c, i, hop], z_dev[dr])

    def q_send(c, hop, dr):
        i = 0 if hop == 0 else 2 * hop - 1 + (dr < 0)
        b = row_of(-dr * hop)
        ref = pvt.at[c, block(b), :]
        qc[c, i] = send(ref, ref, q_ss.at[c, i], q_rs.at[c, i], partner)

    vc = {}

    def spread(c):
        precv[c, l] = pst[c, 0:PB, :]
        for d in (2, 1, 3):
            vc[c, d] = send(
                pst.at[c, pl.ds(0, PB), :], precv.at[c, l], v_ss.at[c, d - 1], v_rs.at[c, d - 1], (layer_of(d), r, x)
            )

    def pivots(c, hop):
        if hop == 0:
            if c == 0:
                loads["top"].wait()
            for d in (1, 2, 3):
                vc[c, d].wait_recv()
            total = v_top[:, c * CW : c * CW + CW]
            for d in range(NL):
                total = total + precv[c, d].astype(F32)
            pvt[c, block(r), :] = total.astype(BF)
            p_send(c, 0, 1)
            p_send(c, 0, -1)
            q_send(c, 0, 0)
            return
        for dr in (1, -1):
            if hop == 4 and dr < 0:
                continue
            pc[c, dr, hop - 1].wait_recv()
            if hop < 3 or (hop == 3 and dr > 0):
                p_send(c, hop, dr)
            q_send(c, hop, dr)

    def anc_low():
        loads["aui"].wait()
        gathered(0)
        gathered(1)

        @pl.when(x == 0)
        def _():
            low = jnp.dot(asum[0], v_aui[0:CW, :], preferred_element_type=F32)
            low = low + jnp.dot(asum[1], v_aui[CW : 2 * CW, :], preferred_element_type=F32)
            v_low[...] = low.astype(BF)
            for d in (2, 1, 3):
                low_copy(d).start()

    def low_copy(d):
        return pltpu.make_async_remote_copy(
            src_ref=v_low,
            dst_ref=v_low,
            send_sem=l_ss.at[d - 1],
            recv_sem=l_rs,
            device_id=(l, r, col_of(d)),
            device_id_type=MESH,
        )

    def low_done():
        @pl.when(x != 0)
        def _():
            low_copy(1).wait_recv()

        @pl.when(x == 0)
        def _():
            for d in (1, 2, 3):
                low_copy(d).wait_send()

    def finish(c):
        for i in range(8):
            qc[c, i].wait_recv()
        gathered(c)
        v_up[c] = jnp.dot(v_alip[...], pvt[c], preferred_element_type=F32).astype(BF)
        prod = jnp.dot(v_low[...], v_up[c], preferred_element_type=F32)
        for p in range(3):
            tile = s_atiles[(3 * r + p) // 2, NC * x + c].astype(F32)
            rows = slice(128 * p, 128 * p + 128)
            v_sch[c, rows, :] = asum[c, rows, :].astype(F32) - tile * prod[rows, :]

    def comp(c):
        ready(c)
        products(c, 0)
        spread(c)
        products(c, 1)
        products(c, 2)
        scatter(c)

    def m_ready():
        x_done()
        loads["tiles"].wait()

    events = {}

    def at(g, fn, *args):
        events.setdefault(g, []).append((fn, args))

    at(1, left_factor, 0)
    at(2, left_factor, 1)
    at(5, anc_left)
    at(10, x_relay)
    at(20, m_ready)
    for c in range(NC):
        at(PLACE[c, 2, 1] + GAP, z_last, c, 2)
        at(PLACE[c, 3, 0] + GAP, z_last, c, 3)
    for c, g in ((0, 20), (1, 22), (2, 30), (3, 33)):
        at(g, comp, c)
    for c, g in ((0, 25), (1, 27), (2, 34), (3, 37)):
        at(g, pivots, c, 0)
        at(g, add_up, c)
    for c, hop, g in ((0, 1, 32), (1, 1, 33), (0, 2, 38), (1, 2, 39)):
        at(g, pivots, c, hop)
    at(31, anc_low)

    n = len(ORDER)
    for g in range(n):
        if ORDER[g] is not None:
            z_send(*ORDER[g])
        for fn, args in events.pop(g, []):
            fn(*args)
    for g in sorted(events):
        for fn, args in events[g]:
            fn(*args)
            if fn is z_last and args == (4, 3):
                comp(4)
                loads["atiles"].wait()
    pivots(0, 3)
    pivots(1, 3)
    pivots(2, 1)
    pivots(3, 1)
    pivots(4, 0)
    comp(5)
    add_up(4)
    pivots(0, 4)
    pivots(1, 4)
    low_done()
    finish(0)
    pivots(2, 2)
    pivots(3, 2)
    pivots(5, 0)
    pivots(4, 1)
    add_up(5)
    finish(1)
    pivots(2, 3)
    pivots(3, 3)
    pivots(5, 1)
    pivots(4, 2)
    pivots(2, 4)
    pivots(3, 4)
    finish(2)
    pivots(5, 2)
    pivots(4, 3)
    finish(3)
    pivots(4, 4)
    pivots(5, 3)
    finish(4)
    pivots(5, 4)
    finish(5)
    for cp in sent:
        cp.wait_send()


def write_out(v_low, v_up, v_sch, o_low, o_up, o_sch, sem):
    copies = [pltpu.make_async_copy(v_low, o_low, sem.at[2 * NC])]
    for c in range(NC):
        cols = pl.ds(c * CW, CW)
        copies.append(pltpu.make_async_copy(v_sch.at[c], o_sch.at[:, cols], sem.at[c]))
        copies.append(pltpu.make_async_copy(v_up.at[c], o_up.at[:, cols], sem.at[NC + c]))
    for cp in copies:
        cp.start()
    for cp in copies:
        cp.wait()


def shards(*args):
    any_space = pl.BlockSpec(memory_space=pl.ANY)
    dma = pltpu.SemaphoreType.DMA
    vmem = pltpu.VMEM
    made = pl.pallas_call(
        kernel,
        out_shape=(vmem((RB, W), BF), vmem((NC, W, CW), BF), vmem((NC, RB, CW), F32)),
        in_specs=[any_space] * 11,
        out_specs=(pl.BlockSpec(memory_space=vmem),) * 3,
        scratch_shapes=[
            vmem((NC, LEAVES, W, CW), BF),
            vmem((LEAVES, RB, W), BF),
            vmem((2, RB, W), BF),
            vmem((2, W, W), BF),
            vmem((2, W, W), BF),
            vmem((W, W), BF),
            vmem((W, W), BF),
            vmem((W, W), BF),
            vmem((LEAVES, W), jnp.int32),
            vmem((1, W), jnp.int32),
            vmem((OWN, CB), F32),
            vmem((NC, RB, CW), F32),
            vmem((NC, RB, CW), BF),
            vmem((NC, 3, OWN, CW), BF),
            vmem((NC, RB, CW), BF),
            vmem((NC, W, CW), BF),
            vmem((PB, CB), F32),
            vmem((NC, NL, PB, CW), BF),
            pltpu.SMEM((LEAVES, 24, 24), jnp.int32),
            pltpu.SMEM((24, 24), jnp.int32),
            dma((11,)),
            dma((NC,)),
            dma((NC, 2, 7)),
            dma((NC, 2, 7)),
            dma((NC, 8)),
            dma((NC, 8)),
            dma((2, 3)),
            dma((2, 3)),
            dma((NC, 3)),
            dma((NC, 3)),
            dma((NC, 3)),
            dma((NC, 3)),
            dma((NC, 2, 4)),
            dma((NC, 2, 4)),
            dma((NC, 8)),
            dma((NC, 8)),
            dma((3,)),
            dma(()),
            dma((NC, 3)),
            dma((NC, 3)),
        ],
        compiler_params=pltpu.CompilerParams(
            collective_id=0, has_side_effects=True, vmem_limit_bytes=56 * 2**20
        ),
    )(*args[:9], args[9].reshape(1, W), args[10])
    return pl.pallas_call(
        write_out,
        out_shape=(
            jax.ShapeDtypeStruct((RB, W), BF),
            jax.ShapeDtypeStruct((W, CB), BF),
            jax.ShapeDtypeStruct((RB, CB), F32),
        ),
        in_specs=[any_space] * 3,
        out_specs=(any_space,) * 3,
        scratch_shapes=[dma((2 * NC + 1,))],
        compiler_params=pltpu.CompilerParams(vmem_limit_bytes=2**20),
    )(*made)


def solution(mesh):
    return jax.shard_map(
        shards,
        mesh=mesh,
        in_specs=(
            P("row", "col"),
            P("layer", "col", "row", None),
            P("layer", None, "row", "col"),
            P("layer", "col", None, None),
            P("layer", None, None, None),
            P("layer", None, None),
            P("layer", None, None, None),
            P(),
            P(),
            P(),
            P(),
        ),
        out_specs=(P("row", None), P(None, "col"), P("row", "col")),
        check_vma=False,
    )
```

```python
import jax
import jax.numpy as jnp
from jax import lax
from jax.experimental import pallas as pl
from jax.experimental.pallas import tpu as pltpu
from jax.sharding import PartitionSpec as P

MESH = pl.DeviceIdType.MESH
F32 = jnp.float32
BF = jnp.bfloat16
W = 512
TB = 256
LEAVES = 8
NL = 4
NR = 16
NX = 4
NZ = 8
RB = 384
PB = 32
CB = 1536
CW = 256
HW = CW // 2
NC = CB // CW
OWN = RB // NL
GAP = 4


def ring_order():
    left = [(c, h, i) for c in range(NC) for h in range(4) for i in range(2) if h < 3 or i == 0]
    order, place = [], {}
    while left:
        g = len(order)
        fit = [m for m in left if m[1] == 0 or place.get((m[0], m[1] - 1, m[2]), g) + GAP <= g]
        order.append(fit[0] if fit else None)
        if fit:
            place[fit[0]] = g
            left.remove(fit[0])
    return order, place


ORDER, PLACE = ring_order()


def kernel(
    anc,
    ll,
    lu,
    lui,
    lli,
    piv,
    tiles,
    aui,
    ali,
    apiv,
    atiles,
    v_low,
    v_up,
    v_sch,
    ubuf,
    mbuf,
    v_ll,
    v_lui,
    v_lli,
    v_aui,
    v_ali,
    v_alip,
    v_piv,
    v_apiv,
    v_anc,
    part,
    pst,
    rrecv,
    asum,
    single,
    pair,
    ppart,
    v_top,
    precv,
    s_tiles,
    s_atiles,
    in_sem,
    own_sem,
    z_ss,
    z_rs,
    d_ss,
    d_rs,
    x_ss,
    x_rs,
    r_ss,
    r_rs,
    a_ss,
    a_rs,
    p_ss,
    p_rs,
    q_ss,
    q_rs,
    l_ss,
    l_rs,
    v_ss,
    v_rs,
    y_ss,
    y_rs,
):
    l = lax.axis_index("layer")
    r = lax.axis_index("row")
    x = lax.axis_index("col")

    def row_of(step):
        return lax.rem(r + (2 * step + 2 * NR), NR)

    z_dev = {1: (l, row_of(1), x), -1: (l, row_of(-1), x)}
    core = lax.rem(r, 2)
    partner = (l, r + 1 - 2 * core, x)
    own_pivots = pl.ds(pl.multiple_of(PB * (r // 2), PB), PB)

    def layer_of(d):
        return lax.rem(l + d, NL)

    def col_of(d):
        return lax.rem(x + d + NX, NX)

    loads = {}

    def load(name, src, dst, index):
        loads[name] = pltpu.make_async_copy(src, dst, in_sem.at[index])
        loads[name].start()

    for c in range(NC):
        cp = pltpu.make_async_copy(
            lu.at[0, :, :, pl.ds(c * CW, CW)],
            ubuf.at[c, :, pl.ds(pl.multiple_of(r * PB, PB), PB), :],
            own_sem.at[c],
        )
        cp.start()
        loads[("own", c)] = cp
    load("ll", ll.at[0], v_ll, 0)
    load("lui", lui.at[0], v_lui, 1)
    load("lli", lli.at[0, pl.ds(2 * x, 2)], v_lli, 2)
    load("piv", piv.at[0], v_piv, 3)
    load("tiles", tiles.at[0], s_tiles, 4)
    load("aui", aui, v_aui, 5)
    load("ali", ali, v_ali, 6)
    load("apiv", apiv, v_apiv, 7)
    load("atiles", atiles, s_atiles, 8)
    load("top", anc.at[pl.ds(0, PB), :], v_top, 10)
    load("anc", anc.at[pl.ds(pl.multiple_of(l * OWN, OWN), OWN), :], v_anc, 9)

    barrier = pltpu.get_barrier_semaphore()
    others = [(l, row_of(d), x) for d in range(1, NZ)] + [partner]
    others += [(layer_of(d), r, x) for d in (1, 2, 3)]
    others += [(l, r, col_of(d)) for d in (1, 2, 3)]
    for dev in others:
        pl.semaphore_signal(barrier, inc=1, device_id=dev, device_id_type=MESH)
    pl.semaphore_wait(barrier, len(others))

    sent = []

    def send(src, dst, ss, rs, dev):
        cp = pltpu.make_async_remote_copy(
            src_ref=src, dst_ref=dst, send_sem=ss, recv_sem=rs, device_id=dev, device_id_type=MESH
        )
        cp.start()
        sent.append(cp)
        return cp

    zc = {}
    dc = {}

    def block(b):
        return pl.ds(pl.multiple_of(b * PB, PB), PB)

    def z_send(c, hop, i):
        for dr in (1, -1):
            n = 0 if dr > 0 else 1
            if hop:
                zc[c, dr, hop - 1, i].wait_recv()
            h = i if dr > 0 else 1 - i
            dst = ubuf.at[c, pl.ds(4 * h, 4), block(row_of(-dr * hop)), :]
            src = lu.at[0, pl.ds(4 * h, 4), :, pl.ds(c * CW, CW)] if hop == 0 else dst
            slot = 2 * hop + i
            zc[c, dr, hop, i] = send(src, dst, z_ss.at[c, n, slot], z_rs.at[c, n, slot], z_dev[dr])
        if hop == 0 and i == 0:
            d_send(c, 0, 0)
        if hop in (1, 2) and i == 1:
            d_send(c, hop, 1)
            d_send(c, hop, -1)

    def d_send(c, hop, dr):
        i = 0 if hop == 0 else (7 if hop == 4 else 2 * hop - 1 + (dr < 0))
        b = row_of(-dr * hop)
        dst = ubuf.at[c, :, block(b), :]
        src = lu.at[0, :, :, pl.ds(c * CW, CW)] if hop == 0 else dst
        dc[c, i] = send(src, dst, d_ss.at[c, i], d_rs.at[c, i], partner)

    def z_last(c, hop):
        for dr in (1, -1):
            zc[c, dr, hop, 1 if hop == 2 else 0].wait_recv()
        if hop == 2:
            d_send(c, 3, 1)
            d_send(c, 3, -1)
        else:
            d_send(c, 4, 1)

    xc = {}

    def onehot_rows(row_vector, by_core=False):
        rows = lax.broadcasted_iota(jnp.int32, (W, W), 0)
        if by_core:
            place = rows % (W // 2)
            rows = 2 * PB * (place // PB) + PB * (rows // (W // 2)) + rows % PB
        return jnp.where(rows == row_vector, 1.0, 0.0).astype(BF)

    def times_t(a, b):
        return lax.dot_general(a, b, (((1,), (1,)), ((), ())), preferred_element_type=F32)

    def left_factor(j):
        if j == 0:
            for name in ("ll", "lui", "lli", "piv"):
                loads[name].wait()
        k = 2 * x + j
        lower = jnp.dot(v_ll[j], v_lui[j], preferred_element_type=F32).astype(BF)
        both = jnp.dot(lower, v_lli[j], preferred_element_type=F32).astype(BF)
        mbuf[k] = times_t(both, onehot_rows(v_piv[pl.ds(k, 1), :])).astype(BF)
        if j == 1:
            x_send(-1, 0, k)
            x_send(-1, 1, k - 1)
        x_send(1, j, k)

    def x_send(dr, slot, k):
        i = 0 if dr > 0 else 1
        ref = mbuf.at[k]
        xc[dr, slot] = send(ref, ref, x_ss.at[i, slot], x_rs.at[i, slot], (l, r, col_of(dr)))

    def x_relay():
        xc[1, 0].wait_recv()
        x_send(1, 2, 2 * col_of(-1))
        xc[-1, 0].wait_recv()
        x_send(-1, 2, 2 * col_of(1) + 1)

    def x_done():
        for dr in (1, -1):
            for slot in (1, 2):
                xc[dr, slot].wait_recv()

    def anc_left():
        loads["ali"].wait()
        loads["apiv"].wait()
        v_alip[...] = times_t(v_ali[...], onehot_rows(v_apiv[...], True)).astype(BF)

    def ready(c):
        for i in range(8):
            dc[c, i].wait_recv()
        loads["own", c].wait()

    def products(c, p):
        rows = slice(128 * p, 128 * p + 128)
        total = None
        for k in range(LEAVES):
            tile = s_tiles[k, (3 * r + p) // 2, NC * x + c].astype(F32)
            prod = tile * jnp.dot(mbuf[k, rows, :], ubuf[c, k], preferred_element_type=F32)
            total = prod if total is None else total + prod
        part[c, rows, :] = total
        pst[c, rows, :] = total.astype(BF)

    rc = {}
    ac = {}

    def own_rows(layer):
        return pl.ds(pl.multiple_of(layer * OWN, OWN), OWN)

    def scatter(c):
        for d in (2, 1, 3):
            to = layer_of(d)
            rc[c, d] = send(
                pst.at[c, own_rows(to), :], rrecv.at[c, d - 1], r_ss.at[c, d - 1], r_rs.at[c, d - 1], (to, r, x)
            )

    def add_up(c):
        if c == 0:
            loads["anc"].wait()
        for d in (1, 2, 3):
            rc[c, d].wait_recv()
        total = part[c, own_rows(l), :] + v_anc[:, c * CW : c * CW + CW]
        for d in range(3):
            total = total + rrecv[c, d].astype(F32)
        asum[c, own_rows(l), :] = total.astype(BF)
        ref = asum.at[c, own_rows(l), :]
        for d in (2, 1, 3):
            ac[c, d] = send(ref, ref, a_ss.at[c, d - 1], a_rs.at[c, d - 1], (layer_of(d), r, x))

    def gathered(c):
        if c not in done:
            done.add(c)
            for d in (1, 2, 3):
                ac[c, d].wait_recv()

    done = set()

    pc = {}
    qc = {}

    def p_send(c, hop, dr):
        i = 0 if dr > 0 else 1
        b = row_of(-dr * hop)
        ref = pvt.at[c, block(b), :]
        pc[c, dr, hop] = send(ref, ref, p_ss.at[c, i, hop], p_rs.at[c, i, hop], z_dev[dr])

    def q_send(c, hop, dr):
        i = 0 if hop == 0 else 2 * hop - 1 + (dr < 0)
        b = row_of(-dr * hop)
        ref = pvt.at[c, block(b), :]
        qc[c, i] = send(ref, ref, q_ss.at[c, i], q_rs.at[c, i], partner)

    vc = {}
    gc = {}
    yc = {}
    qc = {}
    to_z = (4, 3, 5, 2, 6, 1, 7)

    def along_z(n, ref):
        for d in to_z:
            gc[n, d] = send(ref, ref, p_ss.at[n, d - 1], p_rs.at[n, d - 1], (l, row_of(d), x))

    def along_z_done(n):
        for d in to_z:
            gc[n, d].wait_recv()

    def to_partner(n, ref):
        qc[n] = send(ref, ref, q_ss.at[n], q_rs.at[n], partner)

    def pair_piece(i, layer):
        return 2 * i + layer // 2, pl.ds(pl.multiple_of(HW * lax.rem(layer, 2), HW), HW)

    def pair_spread(i):
        c, cols = pair_piece(i, l)
        ppart[i, l] = pst[c, 0:PB, cols]
        for d in (2, 1, 3):
            to = layer_of(d)
            c, cols = pair_piece(i, to)
            vc[i, d] = send(
                pst.at[c, pl.ds(0, PB), cols], ppart.at[i, l], v_ss.at[i, d - 1], v_rs.at[i, d - 1], (to, r, x)
            )

    def pair_sum(i):
        if i == 0:
            loads["top"].wait()
        for d in (1, 2, 3):
            vc[i, d].wait_recv()
        total = v_top[:, pl.ds(pl.multiple_of(2 * CW * i + HW * l, HW), HW)]
        for d in range(NL):
            total = total + ppart[i, d].astype(F32)
        pair[i, core, l, own_pivots, :] = total.astype(BF)
        along_z(i, pair.at[i, core, l, own_pivots, :])

    def pair_layers(i):
        along_z_done(i)
        ref = pair.at[i, core, l]
        for d in (2, 1, 3):
            yc[i, d] = send(ref, ref, y_ss.at[i, d - 1], y_rs.at[i, d - 1], (layer_of(d), r, x))

    def pair_partner(i):
        for d in (1, 2, 3):
            yc[i, d].wait_recv()
        to_partner(i, pair.at[i, core])

    def spread(c):
        i = c - 2
        precv[c - 4, l] = pst[c, 0:PB, :]
        for d in (2, 1, 3):
            vc[i, d] = send(
                pst.at[c, pl.ds(0, PB), :], precv.at[c - 4, l], v_ss.at[i, d - 1], v_rs.at[i, d - 1], (layer_of(d), r, x)
            )

    def single_sum(c):
        for d in (1, 2, 3):
            vc[c - 2, d].wait_recv()
        total = v_top[:, c * CW : c * CW + CW]
        for d in range(NL):
            total = total + precv[c - 4, d].astype(F32)
        single[c - 4, core, own_pivots, :] = total.astype(BF)
        along_z(c - 2, single.at[c - 4, core, own_pivots, :])

    def single_partner(c):
        along_z_done(c - 2)
        to_partner(c - 2, single.at[c - 4, core])

    def gathered(c):
        if c not in done:
            done.add(c)
            for d in (1, 2, 3):
                ac[c, d].wait_recv()

    def pivot_rows(c, of_core):
        if c >= 4:
            return single[c - 4, of_core]
        i, e = c // 2, 2 * (c % 2)
        return jnp.concatenate([pair[i, of_core, e], pair[i, of_core, e + 1]], axis=1)

    done = set()
    met = set()

    def anc_low():
        loads["aui"].wait()
        gathered(0)
        gathered(1)

        @pl.when(x == 0)
        def _():
            low = jnp.dot(asum[0], v_aui[0:CW, :], preferred_element_type=F32)
            low = low + jnp.dot(asum[1], v_aui[CW : 2 * CW, :], preferred_element_type=F32)
            v_low[...] = low.astype(BF)
            for d in (2, 1, 3):
                low_copy(d).start()

    def low_copy(d):
        return pltpu.make_async_remote_copy(
            src_ref=v_low,
            dst_ref=v_low,
            send_sem=l_ss.at[d - 1],
            recv_sem=l_rs,
            device_id=(l, r, col_of(d)),
            device_id_type=MESH,
        )

    def low_done():
        @pl.when(x != 0)
        def _():
            low_copy(1).wait_recv()

        @pl.when(x == 0)
        def _():
            for d in (1, 2, 3):
                low_copy(d).wait_send()

    def finish(c):
        n = c // 2 if c < 4 else c - 2
        if n not in met:
            met.add(n)
            qc[n].wait_recv()
        gathered(c)
        half = W // 2
        up = jnp.dot(v_alip[:, 0:half], pivot_rows(c, 0), preferred_element_type=F32)
        up = up + jnp.dot(v_alip[:, half:W], pivot_rows(c, 1), preferred_element_type=F32)
        v_up[c] = up.astype(BF)
        prod = jnp.dot(v_low[...], v_up[c], preferred_element_type=F32)
        for p in range(3):
            tile = s_atiles[(3 * r + p) // 2, NC * x + c].astype(F32)
            rows = slice(128 * p, 128 * p + 128)
            v_sch[c, rows, :] = asum[c, rows, :].astype(F32) - tile * prod[rows, :]

    def comp(c):
        ready(c)
        products(c, 0)
        if c >= 4:
            spread(c)
        elif c % 2:
            pair_spread(c // 2)
        products(c, 1)
        products(c, 2)
        scatter(c)

    def m_ready():
        x_done()
        loads["tiles"].wait()

    events = {}

    def at(g, fn, *args):
        events.setdefault(g, []).append((fn, args))

    at(1, left_factor, 0)
    at(2, left_factor, 1)
    at(5, anc_left)
    at(10, x_relay)
    at(20, m_ready)
    for c in range(NC):
        at(PLACE[c, 2, 1] + GAP, z_last, c, 2)
        at(PLACE[c, 3, 0] + GAP, z_last, c, 3)
    for c, g in ((0, 20), (1, 22), (2, 30), (3, 33)):
        at(g, comp, c)
    for c, g in ((0, 25), (1, 27), (2, 34), (3, 38)):
        at(g, add_up, c)
    at(26, pair_sum, 0)
    at(32, pair_layers, 0)
    at(36, pair_partner, 0)
    at(37, pair_sum, 1)
    at(31, anc_low)

    n = len(ORDER)
    for g in range(n):
        if ORDER[g] is not None:
            z_send(*ORDER[g])
        for fn, args in events.pop(g, []):
            fn(*args)
    for g in sorted(events):
        for fn, args in events[g]:
            fn(*args)
            if fn is z_last and args == (4, 3):
                comp(4)
                loads["atiles"].wait()
    pair_layers(1)
    single_sum(4)
    comp(5)
    add_up(4)
    pair_partner(1)
    low_done()
    finish(0)
    single_sum(5)
    add_up(5)
    finish(1)
    finish(2)
    finish(3)
    single_partner(4)
    finish(4)
    single_partner(5)
    finish(5)
    for cp in sent:
        cp.wait_send()


def write_out(v_low, v_up, v_sch, o_low, o_up, o_sch, sem):
    copies = [pltpu.make_async_copy(v_low, o_low, sem.at[2 * NC])]
    for c in range(NC):
        cols = pl.ds(c * CW, CW)
        copies.append(pltpu.make_async_copy(v_sch.at[c], o_sch.at[:, cols], sem.at[c]))
        copies.append(pltpu.make_async_copy(v_up.at[c], o_up.at[:, cols], sem.at[NC + c]))
    for cp in copies:
        cp.start()
    for cp in copies:
        cp.wait()


def shards(*args):
    any_space = pl.BlockSpec(memory_space=pl.ANY)
    dma = pltpu.SemaphoreType.DMA
    vmem = pltpu.VMEM
    made = pl.pallas_call(
        kernel,
        out_shape=(vmem((RB, W), BF), vmem((NC, W, CW), BF), vmem((NC, RB, CW), F32)),
        in_specs=[any_space] * 11,
        out_specs=(pl.BlockSpec(memory_space=vmem),) * 3,
        scratch_shapes=[
            vmem((NC, LEAVES, W, CW), BF),
            vmem((LEAVES, RB, W), BF),
            vmem((2, RB, W), BF),
            vmem((2, W, W), BF),
            vmem((2, W, W), BF),
            vmem((W, W), BF),
            vmem((W, W), BF),
            vmem((W, W), BF),
            vmem((LEAVES, W), jnp.int32),
            vmem((1, W), jnp.int32),
            vmem((OWN, CB), F32),
            vmem((NC, RB, CW), F32),
            vmem((NC, RB, CW), BF),
            vmem((NC, 3, OWN, CW), BF),
            vmem((NC, RB, CW), BF),
            vmem((2, 2, W // 2, CW), BF),
            vmem((2, 2, NL, W // 2, HW), BF),
            vmem((2, NL, PB, HW), BF),
            vmem((PB, CB), F32),
            vmem((2, NL, PB, CW), BF),
            pltpu.SMEM((LEAVES, 24, 24), jnp.int32),
            pltpu.SMEM((24, 24), jnp.int32),
            dma((11,)),
            dma((NC,)),
            dma((NC, 2, 7)),
            dma((NC, 2, 7)),
            dma((NC, 8)),
            dma((NC, 8)),
            dma((2, 3)),
            dma((2, 3)),
            dma((NC, 3)),
            dma((NC, 3)),
            dma((NC, 3)),
            dma((NC, 3)),
            dma((4, NZ - 1)),
            dma((4, NZ - 1)),
            dma((4,)),
            dma((4,)),
            dma((3,)),
            dma(()),
            dma((4, 3)),
            dma((4, 3)),
            dma((2, 3)),
            dma((2, 3)),
        ],
        compiler_params=pltpu.CompilerParams(
            collective_id=0, has_side_effects=True, vmem_limit_bytes=56 * 2**20
        ),
    )(*args[:9], args[9].reshape(1, W), args[10])
    return pl.pallas_call(
        write_out,
        out_shape=(
            jax.ShapeDtypeStruct((RB, W), BF),
            jax.ShapeDtypeStruct((W, CB), BF),
            jax.ShapeDtypeStruct((RB, CB), F32),
        ),
        in_specs=[any_space] * 3,
        out_specs=(any_space,) * 3,
        scratch_shapes=[dma((2 * NC + 1,))],
        compiler_params=pltpu.CompilerParams(vmem_limit_bytes=2**20),
    )(*made)


def solution(mesh):
    return jax.shard_map(
        shards,
        mesh=mesh,
        in_specs=(
            P("row", "col"),
            P("layer", "col", "row", None),
            P("layer", None, "row", "col"),
            P("layer", "col", None, None),
            P("layer", None, None, None),
            P("layer", None, None),
            P("layer", None, None, None),
            P(),
            P(),
            P(),
            P(),
        ),
        out_specs=(P("row", None), P(None, "col"), P("row", "col")),
        check_vma=False,
    )
```

```python
import jax
import jax.numpy as jnp
from jax import lax
from jax.experimental import pallas as pl
from jax.experimental.pallas import tpu as pltpu
from jax.sharding import PartitionSpec as P

MESH = pl.DeviceIdType.MESH
F32 = jnp.float32
BF = jnp.bfloat16
W = 512
TB = 256
LEAVES = 8
NL = 4
NR = 16
NX = 4
NZ = 8
RB = 384
PB = 32
CB = 1536
CW = 256
HW = CW // 2
WIDTHS = (256, 256, 256, 256, 256, 256)
NC = len(WIDTHS)
FIRST = [sum(WIDTHS[:c]) for c in range(NC)]
OWN = RB // NL
LAG = 3.0


def ring_order():
    left = [(c, h, i) for c in range(NC) for h in range(4) for i in range(2) if h < 3 or i == 0]
    start, t = {}, 0.0
    while left:
        fit = [
            (c, h, i)
            for c, h, i in left
            if h == 0 or ((c, h - 1, i) in start and start[c, h - 1, i] + WIDTHS[c] / CW + LAG <= t)
        ]
        if fit:
            start[fit[0]] = t
            left.remove(fit[0])
            t += WIDTHS[fit[0][0]] / CW
        else:
            t += 0.25
    return start


START = ring_order()


def spans(c):
    return pl.ds(FIRST[c], WIDTHS[c])


def span(c):
    return pl.ds(0, WIDTHS[c])


def kernel(
    anc,
    ll,
    lu,
    lui,
    lli,
    piv,
    tiles,
    aui,
    ali,
    apiv,
    atiles,
    v_low,
    v_up,
    v_sch,
    ubuf,
    mbuf,
    v_ll,
    v_lui,
    v_lli,
    v_aui,
    v_ali,
    v_alip,
    v_piv,
    v_apiv,
    v_anc,
    part,
    pst,
    rrecv,
    asum,
    single,
    pair,
    ppart,
    v_top,
    precv,
    s_tiles,
    s_atiles,
    in_sem,
    own_sem,
    z_ss,
    z_rs,
    d_ss,
    d_rs,
    x_ss,
    x_rs,
    r_ss,
    r_rs,
    a_ss,
    a_rs,
    p_ss,
    p_rs,
    q_ss,
    q_rs,
    l_ss,
    l_rs,
    v_ss,
    v_rs,
    y_ss,
    y_rs,
):
    l = lax.axis_index("layer")
    r = lax.axis_index("row")
    x = lax.axis_index("col")

    def row_of(step):
        return lax.rem(r + (2 * step + 2 * NR), NR)

    z_dev = {1: (l, row_of(1), x), -1: (l, row_of(-1), x)}
    core = lax.rem(r, 2)
    partner = (l, r + 1 - 2 * core, x)
    own_pivots = pl.ds(pl.multiple_of(PB * (r // 2), PB), PB)

    def layer_of(d):
        return lax.rem(l + d, NL)

    def col_of(d):
        return lax.rem(x + d + NX, NX)

    loads = {}

    def load(name, src, dst, index):
        loads[name] = pltpu.make_async_copy(src, dst, in_sem.at[index])
        loads[name].start()

    for c in range(NC):
        cp = pltpu.make_async_copy(
            lu.at[0, :, :, spans(c)],
            ubuf.at[c, :, pl.ds(pl.multiple_of(r * PB, PB), PB), span(c)],
            own_sem.at[c],
        )
        cp.start()
        loads[("own", c)] = cp
    load("ll", ll.at[0], v_ll, 0)
    load("lui", lui.at[0], v_lui, 1)
    load("lli", lli.at[0, pl.ds(2 * x, 2)], v_lli, 2)
    load("piv", piv.at[0], v_piv, 3)
    load("tiles", tiles.at[0], s_tiles, 4)
    load("aui", aui, v_aui, 5)
    load("ali", ali, v_ali, 6)
    load("apiv", apiv, v_apiv, 7)
    load("atiles", atiles, s_atiles, 8)
    load("top", anc.at[pl.ds(0, PB), :], v_top, 10)
    load("anc", anc.at[pl.ds(pl.multiple_of(l * OWN, OWN), OWN), :], v_anc, 9)

    barrier = pltpu.get_barrier_semaphore()
    others = [(l, row_of(d), x) for d in range(1, NZ)] + [partner]
    others += [(layer_of(d), r, x) for d in (1, 2, 3)]
    others += [(l, r, col_of(d)) for d in (1, 2, 3)]
    for dev in others:
        pl.semaphore_signal(barrier, inc=1, device_id=dev, device_id_type=MESH)
    pl.semaphore_wait(barrier, len(others))

    sent = []

    def send(src, dst, ss, rs, dev):
        cp = pltpu.make_async_remote_copy(
            src_ref=src, dst_ref=dst, send_sem=ss, recv_sem=rs, device_id=dev, device_id_type=MESH
        )
        cp.start()
        sent.append(cp)
        return cp

    zc = {}
    dc = {}

    def block(b):
        return pl.ds(pl.multiple_of(b * PB, PB), PB)

    def z_send(c, hop, i):
        for dr in (1, -1):
            n = 0 if dr > 0 else 1
            if hop:
                zc[c, dr, hop - 1, i].wait_recv()
            h = i if dr > 0 else 1 - i
            dst = ubuf.at[c, pl.ds(4 * h, 4), block(row_of(-dr * hop)), span(c)]
            src = lu.at[0, pl.ds(4 * h, 4), :, spans(c)] if hop == 0 else dst
            slot = 2 * hop + i
            zc[c, dr, hop, i] = send(src, dst, z_ss.at[c, n, slot], z_rs.at[c, n, slot], z_dev[dr])
        if hop == 0 and i == 0:
            d_send(c, 0, 0)
        if hop in (1, 2) and i == 1:
            d_send(c, hop, 1)
            d_send(c, hop, -1)

    def d_send(c, hop, dr):
        i = 0 if hop == 0 else (7 if hop == 4 else 2 * hop - 1 + (dr < 0))
        b = row_of(-dr * hop)
        dst = ubuf.at[c, :, block(b), span(c)]
        src = lu.at[0, :, :, spans(c)] if hop == 0 else dst
        dc[c, i] = send(src, dst, d_ss.at[c, i], d_rs.at[c, i], partner)

    def z_last(c, hop):
        for dr in (1, -1):
            zc[c, dr, hop, 1 if hop == 2 else 0].wait_recv()
        if hop == 2:
            d_send(c, 3, 1)
            d_send(c, 3, -1)
        else:
            d_send(c, 4, 1)

    xc = {}

    def onehot_rows(row_vector, by_core=False):
        rows = lax.broadcasted_iota(jnp.int32, (W, W), 0)
        if by_core:
            place = rows % (W // 2)
            rows = 2 * PB * (place // PB) + PB * (rows // (W // 2)) + rows % PB
        return jnp.where(rows == row_vector, 1.0, 0.0).astype(BF)

    def times_t(a, b):
        return lax.dot_general(a, b, (((1,), (1,)), ((), ())), preferred_element_type=F32)

    def left_factor(j):
        if j == 0:
            for name in ("ll", "lui", "lli", "piv"):
                loads[name].wait()
        k = 2 * x + j
        lower = jnp.dot(v_ll[j], v_lui[j], preferred_element_type=F32).astype(BF)
        both = jnp.dot(lower, v_lli[j], preferred_element_type=F32).astype(BF)
        mbuf[k] = times_t(both, onehot_rows(v_piv[pl.ds(k, 1), :])).astype(BF)
        if j == 1:
            x_send(-1, 0, k)
            x_send(-1, 1, k - 1)
        x_send(1, j, k)

    def x_send(dr, slot, k):
        i = 0 if dr > 0 else 1
        ref = mbuf.at[k]
        xc[dr, slot] = send(ref, ref, x_ss.at[i, slot], x_rs.at[i, slot], (l, r, col_of(dr)))

    def x_relay():
        xc[1, 0].wait_recv()
        x_send(1, 2, 2 * col_of(-1))
        xc[-1, 0].wait_recv()
        x_send(-1, 2, 2 * col_of(1) + 1)

    def x_done():
        for dr in (1, -1):
            for slot in (1, 2):
                xc[dr, slot].wait_recv()

    def anc_left():
        loads["ali"].wait()
        loads["apiv"].wait()
        v_alip[...] = times_t(v_ali[...], onehot_rows(v_apiv[...], True)).astype(BF)

    def ready(c):
        for i in range(8):
            dc[c, i].wait_recv()
        loads["own", c].wait()

    def products(c, p):
        rows = slice(128 * p, 128 * p + 128)
        total = None
        for k in range(LEAVES):
            tile = s_tiles[k, (3 * r + p) // 2, CB // TB * x + FIRST[c] // TB].astype(F32)
            prod = tile * jnp.dot(mbuf[k, rows, :], ubuf[c, k, :, span(c)], preferred_element_type=F32)
            total = prod if total is None else total + prod
        part[c, rows, span(c)] = total
        pst[c, rows, span(c)] = total.astype(BF)

    rc = {}
    ac = {}

    def own_rows(layer):
        return pl.ds(pl.multiple_of(layer * OWN, OWN), OWN)

    def scatter(c):
        for d in (2, 1, 3):
            to = layer_of(d)
            rc[c, d] = send(
                pst.at[c, own_rows(to), span(c)],
                rrecv.at[c, d - 1, :, span(c)],
                r_ss.at[c, d - 1],
                r_rs.at[c, d - 1],
                (to, r, x),
            )

    def add_up(c):
        if c == 0:
            loads["anc"].wait()
        for d in (1, 2, 3):
            rc[c, d].wait_recv()
        total = part[c, own_rows(l), span(c)] + v_anc[:, spans(c)]
        for d in range(3):
            total = total + rrecv[c, d, :, span(c)].astype(F32)
        asum[c, own_rows(l), span(c)] = total.astype(BF)
        ref = asum.at[c, own_rows(l), span(c)]
        for d in (2, 1, 3):
            ac[c, d] = send(ref, ref, a_ss.at[c, d - 1], a_rs.at[c, d - 1], (layer_of(d), r, x))

    vc = {}
    gc = {}
    yc = {}
    qc = {}
    to_z = (4, 3, 5, 2, 6, 1, 7)

    def along_z(n, ref):
        for d in to_z:
            gc[n, d] = send(ref, ref, p_ss.at[n, d - 1], p_rs.at[n, d - 1], (l, row_of(d), x))

    def along_z_done(n):
        for d in to_z:
            gc[n, d].wait_recv()

    def to_partner(n, ref):
        qc[n] = send(ref, ref, q_ss.at[n], q_rs.at[n], partner)

    def pair_piece(i, layer):
        return 2 * i + layer // 2, pl.ds(pl.multiple_of(HW * lax.rem(layer, 2), HW), HW)

    def pair_spread(i):
        c, cols = pair_piece(i, l)
        ppart[i, l] = pst[c, 0:PB, cols]
        for d in (2, 1, 3):
            to = layer_of(d)
            c, cols = pair_piece(i, to)
            vc[i, d] = send(
                pst.at[c, pl.ds(0, PB), cols], ppart.at[i, l], v_ss.at[i, d - 1], v_rs.at[i, d - 1], (to, r, x)
            )

    def pair_sum(i):
        if i == 0:
            loads["top"].wait()
        for d in (1, 2, 3):
            vc[i, d].wait_recv()
        total = v_top[:, pl.ds(pl.multiple_of(2 * CW * i + HW * l, HW), HW)]
        for d in range(NL):
            total = total + ppart[i, d].astype(F32)
        pair[i, core, l, own_pivots, :] = total.astype(BF)
        if i == 0:
            pair_hop(0)
        else:
            along_z(i, pair.at[i, core, l, own_pivots, :])

    def pair_hop(hop):
        for dr in (1, -1):
            if hop == 4 and dr < 0:
                continue
            if hop:
                gc[0, dr, hop - 1].wait_recv()
            if hop < 3 or (hop == 3 and dr > 0):
                at_z = lax.rem(r // 2 - dr * hop + NZ, NZ)
                ref = pair.at[0, core, l, pl.ds(pl.multiple_of(PB * at_z, PB), PB), :]
                slot = hop if dr > 0 else 4 + hop
                gc[0, dr, hop] = send(ref, ref, p_ss.at[0, slot], p_rs.at[0, slot], z_dev[dr])

    def pair_layers(i):
        if i:
            along_z_done(i)
        ref = pair.at[i, core, l]
        for d in (2, 1, 3):
            yc[i, d] = send(ref, ref, y_ss.at[i, d - 1], y_rs.at[i, d - 1], (layer_of(d), r, x))

    def pair_partner(i):
        for d in (1, 2, 3):
            yc[i, d].wait_recv()
        to_partner(i, pair.at[i, core])

    def spread(c):
        i = c - 2
        precv[c - 4, l, :, span(c)] = pst[c, 0:PB, span(c)]
        for d in (2, 1, 3):
            vc[i, d] = send(
                pst.at[c, pl.ds(0, PB), span(c)],
                precv.at[c - 4, l, :, span(c)],
                v_ss.at[i, d - 1],
                v_rs.at[i, d - 1],
                (layer_of(d), r, x),
            )

    def single_sum(c):
        for d in (1, 2, 3):
            vc[c - 2, d].wait_recv()
        total = v_top[:, spans(c)]
        for d in range(NL):
            total = total + precv[c - 4, d, :, span(c)].astype(F32)
        single[c - 4, core, own_pivots, span(c)] = total.astype(BF)
        along_z(c - 2, single.at[c - 4, core, own_pivots, span(c)])

    def single_partner(c):
        along_z_done(c - 2)
        to_partner(c - 2, single.at[c - 4, core, :, span(c)])

    def gathered(c):
        if c not in done:
            done.add(c)
            for d in (1, 2, 3):
                ac[c, d].wait_recv()

    def pivot_rows(c, of_core):
        if c >= 4:
            return single[c - 4, of_core, :, span(c)]
        i, e = c // 2, 2 * (c % 2)
        return jnp.concatenate([pair[i, of_core, e], pair[i, of_core, e + 1]], axis=1)

    done = set()
    met = set()

    def anc_low():
        loads["aui"].wait()
        gathered(0)
        gathered(1)

        @pl.when(x == 0)
        def _():
            low = jnp.dot(asum[0], v_aui[0:CW, :], preferred_element_type=F32)
            low = low + jnp.dot(asum[1], v_aui[CW : 2 * CW, :], preferred_element_type=F32)
            v_low[...] = low.astype(BF)
            for d in (2, 1, 3):
                low_copy(d).start()

    def low_copy(d):
        return pltpu.make_async_remote_copy(
            src_ref=v_low,
            dst_ref=v_low,
            send_sem=l_ss.at[d - 1],
            recv_sem=l_rs,
            device_id=(l, r, col_of(d)),
            device_id_type=MESH,
        )

    def low_done():
        @pl.when(x != 0)
        def _():
            low_copy(1).wait_recv()

        @pl.when(x == 0)
        def _():
            for d in (1, 2, 3):
                low_copy(d).wait_send()

    def finish(c):
        n = c // 2 if c < 4 else c - 2
        if n not in met:
            met.add(n)
            qc[n].wait_recv()
        gathered(c)
        half = W // 2
        up = jnp.dot(v_alip[:, 0:half], pivot_rows(c, 0), preferred_element_type=F32)
        up = up + jnp.dot(v_alip[:, half:W], pivot_rows(c, 1), preferred_element_type=F32)
        up = up.astype(BF)
        v_up[c, :, span(c)] = up
        prod = jnp.dot(v_low[...], up, preferred_element_type=F32)
        for p in range(3):
            tile = s_atiles[(3 * r + p) // 2, CB // TB * x + FIRST[c] // TB].astype(F32)
            rows = slice(128 * p, 128 * p + 128)
            v_sch[c, rows, span(c)] = asum[c, rows, span(c)].astype(F32) - tile * prod[rows, :]

    def comp_top(c):
        ready(c)
        products(c, 0)
        if c >= 4:
            spread(c)
        elif c % 2:
            pair_spread(c // 2)

    def comp_low(c):
        products(c, 2)
        scatter(c)

    def comp(c):
        comp_top(c)
        products(c, 1)
        comp_low(c)

    def m_ready():
        x_done()
        loads["tiles"].wait()

    events = []

    def at(t, fn, *args):
        events.append((t, len(events), fn, args))

    at(1, left_factor, 0)
    at(2, left_factor, 1)
    at(5, anc_left)
    at(10, x_relay)
    at(20, m_ready)
    for c in range(NC):
        end = WIDTHS[c] / CW + LAG
        at(max(START[c, 2, 1] + end, START[c, 3, 0]), z_last, c, 2)
        at(START[c, 3, 0] + end, z_last, c, 3)
        if 4 <= c < NC - 1:
            at(START[c, 3, 0] + end, comp, c)
            at(START[c, 3, 0] + end + 2.5, single_sum, c)
            at(START[c, 3, 0] + end + 4, add_up, c)
    for c, t in ((0, 20), (1, 22), (2, START[2, 3, 0] + 1 + LAG), (3, START[3, 3, 0] + 1 + LAG)):
        at(t, comp_top, c)
        at(t + 1, products, c, 1)
        at(t + 2, comp_low, c)
    for c, t in ((0, 27), (1, 29), (2, 35), (3, 38)):
        at(t, add_up, c)
    at(26.5, pair_sum, 0)
    for hop in range(1, 5):
        at(26.5 + 3.5 * hop, pair_hop, hop)
    at(40.5, pair_layers, 0)
    at(43.5, pair_partner, 0)
    at(36, pair_sum, 1)
    at(43.2, pair_layers, 1)
    at(34, anc_low)
    at(40, loads["atiles"].wait)
    events.sort()
    ready_at = START[NC - 1, 3, 0] + WIDTHS[NC - 1] / CW + LAG

    def until(t):
        while events and events[0][0] <= t:
            _, _, fn, args = events.pop(0)
            fn(*args)

    for message, t in sorted(START.items(), key=lambda m: m[1]):
        z_send(*message)
        until(t)
    until(ready_at)
    comp(NC - 1)
    until(100)
    low_done()
    finish(0)
    single_sum(NC - 1)
    pair_partner(1)
    finish(1)
    finish(2)
    add_up(NC - 1)
    finish(3)
    for c in range(4, NC):
        single_partner(c)
        finish(c)
    for cp in sent:
        cp.wait_send()


def write_out(v_low, v_up, v_sch, o_low, o_up, o_sch, sem):
    copies = [pltpu.make_async_copy(v_low, o_low, sem.at[2 * NC])]
    for c in range(NC):
        cols, own = spans(c), span(c)
        copies.append(pltpu.make_async_copy(v_sch.at[c, :, own], o_sch.at[:, cols], sem.at[c]))
        copies.append(pltpu.make_async_copy(v_up.at[c, :, own], o_up.at[:, cols], sem.at[NC + c]))
    for cp in copies:
        cp.start()
    for cp in copies:
        cp.wait()


def shards(*args):
    any_space = pl.BlockSpec(memory_space=pl.ANY)
    dma = pltpu.SemaphoreType.DMA
    vmem = pltpu.VMEM
    made = pl.pallas_call(
        kernel,
        out_shape=(vmem((RB, W), BF), vmem((NC, W, CW), BF), vmem((NC, RB, CW), F32)),
        in_specs=[any_space] * 11,
        out_specs=(pl.BlockSpec(memory_space=vmem),) * 3,
        scratch_shapes=[
            vmem((NC, LEAVES, W, CW), BF),
            vmem((LEAVES, RB, W), BF),
            vmem((2, RB, W), BF),
            vmem((2, W, W), BF),
            vmem((2, W, W), BF),
            vmem((W, W), BF),
            vmem((W, W), BF),
            vmem((W, W), BF),
            vmem((LEAVES, W), jnp.int32),
            vmem((1, W), jnp.int32),
            vmem((OWN, CB), F32),
            vmem((NC, RB, CW), F32),
            vmem((NC, RB, CW), BF),
            vmem((NC, 3, OWN, CW), BF),
            vmem((NC, RB, CW), BF),
            vmem((NC - 4, 2, W // 2, CW), BF),
            vmem((2, 2, NL, W // 2, HW), BF),
            vmem((2, NL, PB, HW), BF),
            vmem((PB, CB), F32),
            vmem((NC - 4, NL, PB, CW), BF),
            pltpu.SMEM((LEAVES, 24, 24), jnp.int32),
            pltpu.SMEM((24, 24), jnp.int32),
            dma((11,)),
            dma((NC,)),
            dma((NC, 2, 7)),
            dma((NC, 2, 7)),
            dma((NC, 8)),
            dma((NC, 8)),
            dma((2, 3)),
            dma((2, 3)),
            dma((NC, 3)),
            dma((NC, 3)),
            dma((NC, 3)),
            dma((NC, 3)),
            dma((NC - 2, NZ - 1)),
            dma((NC - 2, NZ - 1)),
            dma((NC - 2,)),
            dma((NC - 2,)),
            dma((3,)),
            dma(()),
            dma((NC - 2, 3)),
            dma((NC - 2, 3)),
            dma((2, 3)),
            dma((2, 3)),
        ],
        compiler_params=pltpu.CompilerParams(
            collective_id=0, has_side_effects=True, vmem_limit_bytes=56 * 2**20
        ),
    )(*args[:9], args[9].reshape(1, W), args[10])
    return pl.pallas_call(
        write_out,
        out_shape=(
            jax.ShapeDtypeStruct((RB, W), BF),
            jax.ShapeDtypeStruct((W, CB), BF),
            jax.ShapeDtypeStruct((RB, CB), F32),
        ),
        in_specs=[any_space] * 3,
        out_specs=(any_space,) * 3,
        scratch_shapes=[dma((2 * NC + 1,))],
        compiler_params=pltpu.CompilerParams(vmem_limit_bytes=2**20),
    )(*made)


def solution(mesh):
    return jax.shard_map(
        shards,
        mesh=mesh,
        in_specs=(
            P("row", "col"),
            P("layer", "col", "row", None),
            P("layer", None, "row", "col"),
            P("layer", "col", None, None),
            P("layer", None, None, None),
            P("layer", None, None),
            P("layer", None, None, None),
            P(),
            P(),
            P(),
            P(),
        ),
        out_specs=(P("row", None), P(None, "col"), P("row", "col")),
        check_vma=False,
    )
```

```python
import jax
import jax.numpy as jnp
from jax import lax
from jax.experimental import pallas as pl
from jax.experimental.pallas import tpu as pltpu
from jax.sharding import PartitionSpec as P

MESH = pl.DeviceIdType.MESH
F32 = jnp.float32
BF = jnp.bfloat16
W = 512
TB = 256
LEAVES = 8
NL = 4
NR = 16
NX = 4
NZ = 8
RB = 384
PB = 32
CB = 1536
CW = 256
HW = CW // 2
WIDTHS = (256, 256, 256, 256, 256, 256)
NC = len(WIDTHS)
FIRST = [sum(WIDTHS[:c]) for c in range(NC)]
OWN = RB // NL
LAG = 3.0


def ring_order():
    left = [(c, h, i) for c in range(NC) for h in range(4) for i in range(2) if h < 3 or i == 0]
    start, t = {}, 0.0
    while left:
        fit = [
            (c, h, i)
            for c, h, i in left
            if h == 0 or ((c, h - 1, i) in start and start[c, h - 1, i] + WIDTHS[c] / CW + LAG <= t)
        ]
        if fit:
            start[fit[0]] = t
            left.remove(fit[0])
            t += WIDTHS[fit[0][0]] / CW
        else:
            t += 0.25
    return start


START = ring_order()


def spans(c):
    return pl.ds(FIRST[c], WIDTHS[c])


def span(c):
    return pl.ds(0, WIDTHS[c])


def kernel(
    anc,
    ll,
    lu,
    lui,
    lli,
    piv,
    tiles,
    aui,
    ali,
    apiv,
    atiles,
    v_low,
    v_up,
    v_sch,
    ubuf,
    mbuf,
    v_ll,
    v_lui,
    v_lli,
    v_aui,
    v_ali,
    v_alip,
    v_piv,
    v_apiv,
    v_anc,
    part,
    pst,
    rrecv,
    asum,
    single,
    pair,
    ppart,
    v_top,
    precv,
    s_tiles,
    s_atiles,
    in_sem,
    own_sem,
    z_ss,
    z_rs,
    d_ss,
    d_rs,
    x_ss,
    x_rs,
    r_ss,
    r_rs,
    a_ss,
    a_rs,
    p_ss,
    p_rs,
    q_ss,
    q_rs,
    l_ss,
    l_rs,
    v_ss,
    v_rs,
    y_ss,
    y_rs,
):
    l = lax.axis_index("layer")
    r = lax.axis_index("row")
    x = lax.axis_index("col")

    def row_of(step):
        return lax.rem(r + (2 * step + 2 * NR), NR)

    z_dev = {1: (l, row_of(1), x), -1: (l, row_of(-1), x)}
    core = lax.rem(r, 2)
    partner = (l, r + 1 - 2 * core, x)
    own_pivots = pl.ds(pl.multiple_of(PB * (r // 2), PB), PB)

    def layer_of(d):
        return lax.rem(l + d, NL)

    def col_of(d):
        return lax.rem(x + d + NX, NX)

    barrier = pltpu.get_barrier_semaphore()
    others = [(l, row_of(d), x) for d in range(1, NZ)] + [partner]
    others += [(layer_of(d), r, x) for d in (1, 2, 3)]
    others += [(l, r, col_of(d)) for d in (1, 2, 3)]
    for dev in others:
        pl.semaphore_signal(barrier, inc=1, device_id=dev, device_id_type=MESH)

    loads = {}

    def load(name, src, dst, index):
        loads[name] = pltpu.make_async_copy(src, dst, in_sem.at[index])
        loads[name].start()

    for c in range(NC):
        cp = pltpu.make_async_copy(
            lu.at[0, :, :, spans(c)],
            ubuf.at[c, :, pl.ds(pl.multiple_of(r * PB, PB), PB), span(c)],
            own_sem.at[c],
        )
        cp.start()
        loads[("own", c)] = cp
    load("ll", ll.at[0], v_ll, 0)
    load("lui", lui.at[0], v_lui, 1)
    load("lli", lli.at[0, pl.ds(2 * x, 2)], v_lli, 2)
    load("piv", piv.at[0], v_piv, 3)
    load("tiles", tiles.at[0], s_tiles, 4)
    load("aui", aui, v_aui, 5)
    load("ali", ali, v_ali, 6)
    load("apiv", apiv, v_apiv, 7)
    load("atiles", atiles, s_atiles, 8)
    load("top", anc.at[pl.ds(0, PB), :], v_top, 10)
    load("anc", anc.at[pl.ds(pl.multiple_of(l * OWN, OWN), OWN), :], v_anc, 9)

    pl.semaphore_wait(barrier, len(others))

    sent = []

    def send(src, dst, ss, rs, dev):
        cp = pltpu.make_async_remote_copy(
            src_ref=src, dst_ref=dst, send_sem=ss, recv_sem=rs, device_id=dev, device_id_type=MESH
        )
        cp.start()
        sent.append(cp)
        return cp

    zc = {}
    dc = {}

    def block(b):
        return pl.ds(pl.multiple_of(b * PB, PB), PB)

    def z_send(c, hop, i):
        for dr in (1, -1):
            n = 0 if dr > 0 else 1
            if hop:
                zc[c, dr, hop - 1, i].wait_recv()
            h = i if dr > 0 else 1 - i
            dst = ubuf.at[c, pl.ds(4 * h, 4), block(row_of(-dr * hop)), span(c)]
            src = lu.at[0, pl.ds(4 * h, 4), :, spans(c)] if hop == 0 else dst
            slot = 2 * hop + i
            zc[c, dr, hop, i] = send(src, dst, z_ss.at[c, n, slot], z_rs.at[c, n, slot], z_dev[dr])
        if hop == 0 and i == 0:
            d_send(c, 0, 0)
        if hop in (1, 2) and i == 1:
            d_send(c, hop, 1)
            d_send(c, hop, -1)

    def d_send(c, hop, dr):
        i = 0 if hop == 0 else (7 if hop == 4 else 2 * hop - 1 + (dr < 0))
        b = row_of(-dr * hop)
        dst = ubuf.at[c, :, block(b), span(c)]
        src = lu.at[0, :, :, spans(c)] if hop == 0 else dst
        dc[c, i] = send(src, dst, d_ss.at[c, i], d_rs.at[c, i], partner)

    def z_last(c, hop):
        for dr in (1, -1):
            zc[c, dr, hop, 1 if hop == 2 else 0].wait_recv()
        if hop == 2:
            d_send(c, 3, 1)
            d_send(c, 3, -1)
        else:
            d_send(c, 4, 1)

    xc = {}

    def onehot_rows(row_vector, by_core=False):
        rows = lax.broadcasted_iota(jnp.int32, (W, W), 0)
        if by_core:
            place = rows % (W // 2)
            rows = 2 * PB * (place // PB) + PB * (rows // (W // 2)) + rows % PB
        return jnp.where(rows == row_vector, 1.0, 0.0).astype(BF)

    def times_t(a, b):
        return lax.dot_general(a, b, (((1,), (1,)), ((), ())), preferred_element_type=F32)

    def left_factor(j):
        if j == 0:
            for name in ("ll", "lui", "lli", "piv"):
                loads[name].wait()
        k = 2 * x + j
        lower = jnp.dot(v_ll[j], v_lui[j], preferred_element_type=F32).astype(BF)
        both = jnp.dot(lower, v_lli[j], preferred_element_type=F32).astype(BF)
        mbuf[k] = times_t(both, onehot_rows(v_piv[pl.ds(k, 1), :])).astype(BF)
        if j == 1:
            x_send(-1, 0, k)
            x_send(-1, 1, k - 1)
        x_send(1, j, k)

    def x_send(dr, slot, k):
        i = 0 if dr > 0 else 1
        ref = mbuf.at[k]
        xc[dr, slot] = send(ref, ref, x_ss.at[i, slot], x_rs.at[i, slot], (l, r, col_of(dr)))

    def x_relay():
        xc[1, 0].wait_recv()
        x_send(1, 2, 2 * col_of(-1))
        xc[-1, 0].wait_recv()
        x_send(-1, 2, 2 * col_of(1) + 1)

    def x_done():
        for dr in (1, -1):
            for slot in (1, 2):
                xc[dr, slot].wait_recv()

    def anc_left():
        loads["ali"].wait()
        loads["apiv"].wait()
        v_alip[...] = times_t(v_ali[...], onehot_rows(v_apiv[...], True)).astype(BF)

    def ready(c):
        for i in range(8):
            dc[c, i].wait_recv()
        loads["own", c].wait()

    def products(c, p):
        rows = slice(128 * p, 128 * p + 128)
        total = None
        for k in range(LEAVES):
            tile = s_tiles[k, (3 * r + p) // 2, CB // TB * x + FIRST[c] // TB].astype(F32)
            prod = tile * jnp.dot(mbuf[k, rows, :], ubuf[c, k, :, span(c)], preferred_element_type=F32)
            total = prod if total is None else total + prod
        part[c, rows, span(c)] = total
        pst[c, rows, span(c)] = total.astype(BF)

    rc = {}
    ac = {}

    def own_rows(layer):
        return pl.ds(pl.multiple_of(layer * OWN, OWN), OWN)

    def scatter(c):
        for d in (2, 1, 3):
            to = layer_of(d)
            rc[c, d] = send(
                pst.at[c, own_rows(to), span(c)],
                rrecv.at[c, d - 1, :, span(c)],
                r_ss.at[c, d - 1],
                r_rs.at[c, d - 1],
                (to, r, x),
            )

    def add_up(c):
        if c == 0:
            loads["anc"].wait()
        for d in (1, 2, 3):
            rc[c, d].wait_recv()
        total = part[c, own_rows(l), span(c)] + v_anc[:, spans(c)]
        for d in range(3):
            total = total + rrecv[c, d, :, span(c)].astype(F32)
        asum[c, own_rows(l), span(c)] = total.astype(BF)
        ref = asum.at[c, own_rows(l), span(c)]
        for d in (2, 1, 3):
            ac[c, d] = send(ref, ref, a_ss.at[c, d - 1], a_rs.at[c, d - 1], (layer_of(d), r, x))

    vc = {}
    gc = {}
    yc = {}
    qc = {}
    to_z = (4, 3, 5, 2, 6, 1, 7)

    def along_z(n, ref):
        for d in to_z:
            gc[n, d] = send(ref, ref, p_ss.at[n, d - 1], p_rs.at[n, d - 1], (l, row_of(d), x))

    def along_z_done(n):
        for d in to_z:
            gc[n, d].wait_recv()

    def to_partner(n, ref):
        qc[n] = send(ref, ref, q_ss.at[n], q_rs.at[n], partner)

    def pair_piece(i, layer):
        return 2 * i + layer // 2, pl.ds(pl.multiple_of(HW * lax.rem(layer, 2), HW), HW)

    def pair_spread(i):
        c, cols = pair_piece(i, l)
        ppart[i, l] = pst[c, 0:PB, cols]
        for d in (2, 1, 3):
            to = layer_of(d)
            c, cols = pair_piece(i, to)
            vc[i, d] = send(
                pst.at[c, pl.ds(0, PB), cols], ppart.at[i, l], v_ss.at[i, d - 1], v_rs.at[i, d - 1], (to, r, x)
            )

    def pair_sum(i):
        if i == 0:
            loads["top"].wait()
        for d in (1, 2, 3):
            vc[i, d].wait_recv()
        total = v_top[:, pl.ds(pl.multiple_of(2 * CW * i + HW * l, HW), HW)]
        for d in range(NL):
            total = total + ppart[i, d].astype(F32)
        pair[i, core, l, own_pivots, :] = total.astype(BF)
        if i == 0:
            pair_hop(0)
        else:
            along_z(i, pair.at[i, core, l, own_pivots, :])

    def pair_hop(hop):
        for dr in (1, -1):
            if hop == 4 and dr < 0:
                continue
            if hop:
                gc[0, dr, hop - 1].wait_recv()
            if hop < 3 or (hop == 3 and dr > 0):
                at_z = lax.rem(r // 2 - dr * hop + NZ, NZ)
                ref = pair.at[0, core, l, pl.ds(pl.multiple_of(PB * at_z, PB), PB), :]
                slot = hop if dr > 0 else 4 + hop
                gc[0, dr, hop] = send(ref, ref, p_ss.at[0, slot], p_rs.at[0, slot], z_dev[dr])

    def pair_layers(i):
        if i:
            along_z_done(i)
        ref = pair.at[i, core, l]
        for d in (2, 1, 3):
            yc[i, d] = send(ref, ref, y_ss.at[i, d - 1], y_rs.at[i, d - 1], (layer_of(d), r, x))

    def pair_partner(i):
        for d in (1, 2, 3):
            yc[i, d].wait_recv()
        to_partner(i, pair.at[i, core])

    def spread(c):
        i = c - 2
        precv[c - 4, l, :, span(c)] = pst[c, 0:PB, span(c)]
        for d in (2, 1, 3):
            vc[i, d] = send(
                pst.at[c, pl.ds(0, PB), span(c)],
                precv.at[c - 4, l, :, span(c)],
                v_ss.at[i, d - 1],
                v_rs.at[i, d - 1],
                (layer_of(d), r, x),
            )

    def single_sum(c):
        for d in (1, 2, 3):
            vc[c - 2, d].wait_recv()
        total = v_top[:, spans(c)]
        for d in range(NL):
            total = total + precv[c - 4, d, :, span(c)].astype(F32)
        single[c - 4, core, own_pivots, span(c)] = total.astype(BF)
        along_z(c - 2, single.at[c - 4, core, own_pivots, span(c)])

    def single_partner(c):
        along_z_done(c - 2)
        to_partner(c - 2, single.at[c - 4, core, :, span(c)])

    def gathered(c):
        if c not in done:
            done.add(c)
            for d in (1, 2, 3):
                ac[c, d].wait_recv()

    def pivot_rows(c, of_core):
        if c >= 4:
            return single[c - 4, of_core, :, span(c)]
        i, e = c // 2, 2 * (c % 2)
        return jnp.concatenate([pair[i, of_core, e], pair[i, of_core, e + 1]], axis=1)

    done = set()
    met = set()

    def anc_low():
        loads["aui"].wait()
        gathered(0)
        gathered(1)

        @pl.when(x == 0)
        def _():
            low = jnp.dot(asum[0], v_aui[0:CW, :], preferred_element_type=F32)
            low = low + jnp.dot(asum[1], v_aui[CW : 2 * CW, :], preferred_element_type=F32)
            v_low[...] = low.astype(BF)
            for d in (2, 1, 3):
                low_copy(d).start()

    def low_copy(d):
        return pltpu.make_async_remote_copy(
            src_ref=v_low,
            dst_ref=v_low,
            send_sem=l_ss.at[d - 1],
            recv_sem=l_rs,
            device_id=(l, r, col_of(d)),
            device_id_type=MESH,
        )

    def low_done():
        @pl.when(x != 0)
        def _():
            low_copy(1).wait_recv()

        @pl.when(x == 0)
        def _():
            for d in (1, 2, 3):
                low_copy(d).wait_send()

    def finish(c):
        n = c // 2 if c < 4 else c - 2
        if n not in met:
            met.add(n)
            qc[n].wait_recv()
        half = W // 2
        up = jnp.dot(v_alip[:, 0:half], pivot_rows(c, 0), preferred_element_type=F32)
        up = up + jnp.dot(v_alip[:, half:W], pivot_rows(c, 1), preferred_element_type=F32)
        up = up.astype(BF)
        v_up[c, :, span(c)] = up
        prod = jnp.dot(v_low[...], up, preferred_element_type=F32)
        gathered(c)
        for p in range(3):
            tile = s_atiles[(3 * r + p) // 2, CB // TB * x + FIRST[c] // TB].astype(F32)
            rows = slice(128 * p, 128 * p + 128)
            v_sch[c, rows, span(c)] = asum[c, rows, span(c)].astype(F32) - tile * prod[rows, :]

    def comp_top(c):
        ready(c)
        products(c, 0)
        if c >= 4:
            spread(c)
        elif c % 2:
            pair_spread(c // 2)

    def comp_low(c):
        products(c, 2)
        scatter(c)

    def comp(c):
        comp_top(c)
        products(c, 1)
        comp_low(c)

    def m_ready():
        x_done()
        loads["tiles"].wait()

    events = []

    def at(t, fn, *args):
        events.append((t, len(events), fn, args))

    at(3, left_factor, 0)
    at(3, left_factor, 1)
    at(7, anc_left)
    at(10, x_relay)
    at(20, m_ready)
    for c in range(NC):
        end = WIDTHS[c] / CW + LAG
        at(max(START[c, 2, 1] + end, START[c, 3, 0]), z_last, c, 2)
        at(START[c, 3, 0] + end, z_last, c, 3)
        if 4 <= c < NC - 1:
            at(START[c, 3, 0] + end, comp, c)
            at(START[c, 3, 0] + end + 2.5, single_sum, c)
            at(START[c, 3, 0] + end + 4, add_up, c)
    for c, t in ((0, 20), (1, 22), (2, START[2, 3, 0] + 1 + LAG), (3, START[3, 3, 0] + 1 + LAG)):
        at(t, comp_top, c)
        at(t + 1, products, c, 1)
        at(t + 2, comp_low, c)
    for c, t in ((0, 27), (1, 29), (2, 35), (3, 38)):
        at(t, add_up, c)
    at(26.5, pair_sum, 0)
    for hop in range(1, 5):
        at(26.5 + 3.5 * hop, pair_hop, hop)
    at(40.5, pair_layers, 0)
    at(43.5, pair_partner, 0)
    at(36, pair_sum, 1)
    at(43.2, pair_layers, 1)
    at(34, anc_low)
    at(40, loads["atiles"].wait)
    events.sort()
    ready_at = START[NC - 1, 3, 0] + WIDTHS[NC - 1] / CW + LAG

    def until(t):
        while events and events[0][0] <= t:
            _, _, fn, args = events.pop(0)
            fn(*args)

    for message, t in sorted(START.items(), key=lambda m: m[1]):
        z_send(*message)
        until(t)
    until(ready_at)
    comp(NC - 1)
    until(100)
    low_done()
    finish(0)
    single_sum(NC - 1)
    pair_partner(1)
    finish(1)
    finish(2)
    add_up(NC - 1)
    finish(3)
    for c in range(4, NC):
        single_partner(c)
        finish(c)
    for cp in sent:
        cp.wait_send()


def write_out(v_low, v_up, v_sch, o_low, o_up, o_sch, sem):
    copies = [pltpu.make_async_copy(v_low, o_low, sem.at[2 * NC])]
    for c in range(NC):
        cols, own = spans(c), span(c)
        copies.append(pltpu.make_async_copy(v_sch.at[c, :, own], o_sch.at[:, cols], sem.at[c]))
        copies.append(pltpu.make_async_copy(v_up.at[c, :, own], o_up.at[:, cols], sem.at[NC + c]))
    for cp in copies:
        cp.start()
    for cp in copies:
        cp.wait()


def shards(*args):
    any_space = pl.BlockSpec(memory_space=pl.ANY)
    dma = pltpu.SemaphoreType.DMA
    vmem = pltpu.VMEM
    made = pl.pallas_call(
        kernel,
        out_shape=(vmem((RB, W), BF), vmem((NC, W, CW), BF), vmem((NC, RB, CW), F32)),
        in_specs=[any_space] * 11,
        out_specs=(pl.BlockSpec(memory_space=vmem),) * 3,
        scratch_shapes=[
            vmem((NC, LEAVES, W, CW), BF),
            vmem((LEAVES, RB, W), BF),
            vmem((2, RB, W), BF),
            vmem((2, W, W), BF),
            vmem((2, W, W), BF),
            vmem((W, W), BF),
            vmem((W, W), BF),
            vmem((W, W), BF),
            vmem((LEAVES, W), jnp.int32),
            vmem((1, W), jnp.int32),
            vmem((OWN, CB), F32),
            vmem((NC, RB, CW), F32),
            vmem((NC, RB, CW), BF),
            vmem((NC, 3, OWN, CW), BF),
            vmem((NC, RB, CW), BF),
            vmem((NC - 4, 2, W // 2, CW), BF),
            vmem((2, 2, NL, W // 2, HW), BF),
            vmem((2, NL, PB, HW), BF),
            vmem((PB, CB), F32),
            vmem((NC - 4, NL, PB, CW), BF),
            pltpu.SMEM((LEAVES, 24, 24), jnp.int32),
            pltpu.SMEM((24, 24), jnp.int32),
            dma((11,)),
            dma((NC,)),
            dma((NC, 2, 7)),
            dma((NC, 2, 7)),
            dma((NC, 8)),
            dma((NC, 8)),
            dma((2, 3)),
            dma((2, 3)),
            dma((NC, 3)),
            dma((NC, 3)),
            dma((NC, 3)),
            dma((NC, 3)),
            dma((NC - 2, NZ - 1)),
            dma((NC - 2, NZ - 1)),
            dma((NC - 2,)),
            dma((NC - 2,)),
            dma((3,)),
            dma(()),
            dma((NC - 2, 3)),
            dma((NC - 2, 3)),
            dma((2, 3)),
            dma((2, 3)),
        ],
        compiler_params=pltpu.CompilerParams(
            collective_id=0, has_side_effects=True, vmem_limit_bytes=56 * 2**20
        ),
    )(*args[:9], args[9].reshape(1, W), args[10])
    return pl.pallas_call(
        write_out,
        out_shape=(
            jax.ShapeDtypeStruct((RB, W), BF),
            jax.ShapeDtypeStruct((W, CB), BF),
            jax.ShapeDtypeStruct((RB, CB), F32),
        ),
        in_specs=[any_space] * 3,
        out_specs=(any_space,) * 3,
        scratch_shapes=[dma((2 * NC + 1,))],
        compiler_params=pltpu.CompilerParams(vmem_limit_bytes=2**20),
    )(*made)


def solution(mesh):
    return jax.shard_map(
        shards,
        mesh=mesh,
        in_specs=(
            P("row", "col"),
            P("layer", "col", "row", None),
            P("layer", None, "row", "col"),
            P("layer", "col", None, None),
            P("layer", None, None, None),
            P("layer", None, None),
            P("layer", None, None, None),
            P(),
            P(),
            P(),
            P(),
        ),
        out_specs=(P("row", None), P(None, "col"), P("row", "col")),
        check_vma=False,
    )
```
